32 devices in a mesh: rows: 16 (over z, x, core), feat: 2 (over y).
Axes of the slice: x: 2, y: 2, z: 4, core: 2. Of those that a mesh axis runs over, the one named last changes fastest.
Arguments:
- gradients: bfloat16 [16384, 8192], P('rows', 'feat'), may hold values from -2500 to 2500
- queries: bfloat16 [1024, 8192], P('rows', 'feat'), may hold values from -0.09375 to 0.09375
- loss_weight: float32 [16384], P('rows'), may hold values from 0.09 to 1
Outputs:
- standardized: bfloat16 [16384, 1024], P('rows', 'feat')
The draws below stay inside these ranges and needn't reach their ends.
All inputs are finite; a program needn't handle non-finite values.
Results may differ from the reference program's by a relative error of at most 0.019.
Values may be sent and summed in bfloat16 or wider, within the bound.
No kernel may reach another device: no remote copies, remote signals or barrier semaphores. Data moves between devices by JAX's collectives and lax.ppermute only.
A program may use at most 64 MiB of HBM per device.

```python
import math
import jax
import jax.numpy as jnp
from jax import lax

K = 8192
QUERIES = 1024
ROW_DEV = 1024
TOTAL = 16384
N_FEAT = 2


def draw_gradients(key, part):
    key_rows = jax.random.fold_in(key, 11)
    key_cols = jax.random.fold_in(key, 12)
    key_mean = jax.random.fold_in(key, 13)
    key_noise = jax.random.fold_in(key, 14)
    key_tilt = jax.random.fold_in(key, 15)
    key_flip = jax.random.fold_in(key, 16)
    key_phase = jax.random.fold_in(key, 17)
    key_block = jax.random.fold_in(key, 18)
    block_count = TOTAL // ROW_DEV
    rows_uniform = jax.random.uniform(key_rows, (TOTAL, 1), jnp.float32)
    cols_uniform = jax.random.uniform(key_cols, (1, K), jnp.float32)
    tilt_uniform = jax.random.uniform(key_tilt, (TOTAL, 1), jnp.float32, -1.0, 1.0)
    column_shift = jax.random.truncated_normal(key_mean, -4.0, 4.0, (1, K), jnp.float32)
    position = jnp.arange(K, dtype=jnp.float32)[None, :] / K
    column_scale = jnp.exp(math.log(3.0) * position) * jnp.exp(math.log(2.0) * cols_uniform)
    flip_sign = (2 * jax.random.randint(key_flip, (), 0, 2) - 1).astype(jnp.float32)
    phase = jax.random.uniform(key_phase, (), jnp.float32, 0.0, 2.0 * math.pi)
    block_index = jnp.arange(block_count, dtype=jnp.int32)
    parity_sign = (1 - 2 * (block_index % 2)).astype(jnp.float32)
    block_place = (block_index.astype(jnp.float32) + 0.5) / block_count
    block_jitter = jax.random.uniform(key_block, (block_count,), jnp.float32, -1.0, 1.0)
    block_log = 0.6 * flip_sign * parity_sign + 0.6 * jnp.cos(2.0 * math.pi * block_place + phase) + 0.2 * block_jitter
    noise_level = jnp.repeat(jnp.exp(block_log), ROW_DEV, total_repeat_length=TOTAL)[:, None]
    noise = jax.random.truncated_normal(key_noise, -5.0, 5.0, (TOTAL, K), jnp.float32)
    row_scale = jnp.exp(math.log(10.0) * rows_uniform)
    shifted = noise_level * noise + 1.5 * column_shift
    tilt = jnp.exp(math.log(4.0) * tilt_uniform * (position - 0.5))
    return jnp.clip(row_scale * column_scale * tilt * shifted, -2500.0, 2500.0).astype(jnp.bfloat16)


def draw_loss_weight(key, part):
    position = jnp.arange(TOTAL, dtype=jnp.float32) / TOTAL
    trend = jnp.exp(math.log(3.0) * (position - 1.0))
    factor = jax.random.uniform(jax.random.fold_in(key, 21), (TOTAL,), jnp.float32, 0.3, 1.0)
    return (trend * factor).astype(jnp.float32)


def strengthened(result, rng, source, target, shards_of, factor):
    def block_of(dim):
        return (jnp.arange(result.shape[dim]) // (result.shape[dim] // shards_of)).reshape((-1,) + (1,) * (result.ndim - 1 - dim))

    one_side = jax.random.permutation(rng, shards_of)[block_of(target)]
    other_side = (block_of(target) + shards_of // 2) % shards_of
    return jnp.where((block_of(source) == one_side) | (block_of(source) == other_side), factor * result, result)


def block_scale(key, extent, split, low, high):
    factor_of = 1.0
    for dim, blocks in split:
        heights = jax.random.uniform(jax.random.fold_in(jax.random.fold_in(key, 6), dim), (blocks,), jnp.float32, low / len(split), high / len(split))
        factor_of = factor_of * jnp.repeat(jnp.exp(heights), extent[dim] // blocks).reshape((-1,) + (1,) * (len(extent) - 1 - dim))
    return factor_of


def noise_with(own_key, dims, deviation, reach, split, heavy, kind=jnp.bfloat16):
    array = deviation * jax.random.normal(own_key, dims, jnp.float32)
    if split:
        array = array * block_scale(own_key, dims, split, -0.22, 0.18)
    return jnp.clip(strengthened(array, jax.random.fold_in(own_key, 3), *heavy), -reach, reach).astype(kind)


def setup_inputs(seed: int = 0) -> dict:
    splits = jax.random.split(jax.random.key(seed), 4)
    gradients = draw_gradients(jax.random.fold_in(splits[3], 71), 0)
    queries = noise_with(splits[1], (QUERIES, K), K ** -0.5, 0.09375, ((0, 16), (1, 2)), (1, 0, 16, 2.0))
    loss_weight = draw_loss_weight(jax.random.fold_in(splits[3], 71), 0)
    return dict(gradients=gradients, queries=queries, loss_weight=loss_weight)


NORM_EPS = 1e-06
VAR_EPS = 1e-05

def reference(gradients, queries, loss_weight):
    column_width = K // N_FEAT
    squares = lax.optimization_barrier(jnp.sum(jnp.square(gradients.astype(jnp.float32)), axis=1))
    raw = jnp.zeros((TOTAL, QUERIES), jnp.float32)
    for block in range(N_FEAT):
        lower = block * column_width
        upper = lower + column_width
        partial_value = lax.dot_general(gradients[:, lower:upper], queries[:, lower:upper], (((1,), (1,)), ((), ())), preferred_element_type=jnp.float32)
        raw = raw + partial_value.astype(jnp.bfloat16).astype(jnp.float32)
    factor = loss_weight / jnp.sqrt(squares / K + NORM_EPS)
    scored = raw * factor[:, None]
    column_mean = lax.optimization_barrier(jnp.mean(scored, axis=0))
    centered = scored - column_mean[None, :]
    column_var = lax.optimization_barrier(jnp.mean(centered * centered, axis=0))
    return (centered * lax.rsqrt(column_var + VAR_EPS)[None, :]).astype(jnp.bfloat16)
```

```python
import functools

import jax
import jax.numpy as jnp
from jax import lax
from jax.experimental import pallas as pl
from jax.experimental.pallas import tpu as pltpu
from jax.sharding import PartitionSpec as P

NORM_EPS = 1e-06
VAR_EPS = 1e-05
VMEM = pl.BlockSpec(memory_space=pltpu.VMEM)
SMEM = pl.BlockSpec(memory_space=pltpu.SMEM)
NT = (((1,), (1,)), ((), ()))


def plain_body(gradients, queries, loss_weight):
    rows_here = gradients.shape[0]
    total_rows = rows_here * lax.axis_size("rows")
    feature_count = gradients.shape[1] * lax.axis_size("feat")
    local_squares = jnp.sum(jnp.square(gradients.astype(jnp.float32)), axis=1)
    squares = lax.psum(local_squares, "feat")
    product = lax.dot_general(
        gradients,
        lax.all_gather(queries, "rows", axis=0, tiled=True),
        NT,
        preferred_element_type=jnp.float32,
    )
    raw = lax.psum_scatter(
        product.astype(jnp.bfloat16), "feat", scatter_dimension=1, tiled=True
    ).astype(jnp.float32)
    factor = loss_weight / jnp.sqrt(squares / feature_count + NORM_EPS)
    scored = raw * factor[:, None]
    column_mean = lax.psum(jnp.sum(scored, axis=0), "rows") / total_rows
    centered = scored - column_mean[None, :]
    square_sums = lax.psum(jnp.sum(centered * centered, axis=0), "rows")
    column_var = square_sums / total_rows
    return (centered * lax.rsqrt(column_var + VAR_EPS)[None, :]).astype(jnp.bfloat16)


def product_kernel(count, block_rows, with_squares, off_ref, grad_ref, *refs):
    units, rest = refs[:count], refs[count:]
    if with_squares:
        out_ref, square_ref, held = rest
    else:
        out_ref, held = rest
    shard = units[0].shape[0]
    for k in range(count):
        held[pl.ds(pl.multiple_of(off_ref[k], shard), shard), :] = units[k][...]

    def step(i, carry):
        rows = pl.ds(pl.multiple_of(i * block_rows, block_rows), block_rows)
        block = grad_ref[rows, :]
        product = lax.dot_general(block, held[...], NT, preferred_element_type=jnp.float32)
        for b in range(out_ref.shape[0]):
            out_ref[b, rows, :] = product[:, b * 128:(b + 1) * 128].astype(jnp.bfloat16)
        if with_squares:
            wide = block.astype(jnp.float32)
            square_ref[rows, :] = jnp.sum(wide * wide, axis=1, keepdims=True)
        return carry

    lax.fori_loop(0, grad_ref.shape[0] // block_rows, step, 0)


def product_call(gradients, units, offsets, with_squares=False):
    rows, depth = gradients.shape
    shard = units[0].shape[0]
    count = len(units)
    blocks = count * shard // 128
    out_shape = [jax.ShapeDtypeStruct((blocks, rows, 128), jnp.bfloat16)]
    if with_squares:
        out_shape.append(jax.ShapeDtypeStruct((rows, 1), jnp.float32))
    flops = 2 * rows * depth * count * shard
    out = pl.pallas_call(
        functools.partial(product_kernel, count, 256, with_squares),
        out_shape=out_shape,
        in_specs=[SMEM] + [VMEM] * (1 + count),
        out_specs=[VMEM] * len(out_shape),
        scratch_shapes=[pltpu.VMEM((count * shard, depth), jnp.bfloat16)],
        compiler_params=pltpu.CompilerParams(vmem_limit_bytes=24 * 1024 * 1024),
        cost_estimate=pl.CostEstimate(
            flops=flops, bytes_accessed=2 * (rows * depth + count * shard * depth), transcendentals=0
        ),
    )(jnp.stack(offsets).astype(jnp.int32), gradients, *units)
    return out if with_squares else out[0]


def score_kernel(keep_ref, come_ref, factor_ref, scored_ref, stat_ref):
    rows = keep_ref.shape[1]
    for b in range(keep_ref.shape[0]):
        raw = keep_ref[b].astype(jnp.float32) + come_ref[b].astype(jnp.float32)
        scored = raw * factor_ref[...]
        scored_ref[b] = scored
        total = jnp.sum(scored, axis=0, keepdims=True)
        mean = total / rows
        centered = scored - mean
        stat_ref[b, 0:1, :] = mean
        stat_ref[b, 1:2, :] = jnp.sum(centered * centered, axis=0, keepdims=True)


def score_call(keep, come, factor):
    blocks, rows, _ = keep.shape
    return pl.pallas_call(
        score_kernel,
        out_shape=[
            jax.ShapeDtypeStruct((blocks, rows, 128), jnp.float32),
            jax.ShapeDtypeStruct((blocks, 2, 128), jnp.float32),
        ],
        in_specs=[VMEM] * 3,
        out_specs=[VMEM] * 2,
        compiler_params=pltpu.CompilerParams(vmem_limit_bytes=16 * 1024 * 1024),
        cost_estimate=pl.CostEstimate(
            flops=6 * blocks * rows * 128, bytes_accessed=8 * blocks * rows * 128, transcendentals=0
        ),
    )(keep, come, factor)


def finish_kernel(place_ref, stat_ref, *refs):
    parts, out_ref = refs[:-1], refs[-1]
    k = 0
    for part in parts:
        for b in range(part.shape[0]):
            columns = pl.ds(pl.multiple_of(place_ref[k] * 128, 128), 128)
            mean = stat_ref[0:1, columns]
            scale = stat_ref[1:2, columns]
            out_ref[:, columns] = ((part[b] - mean) * scale).astype(jnp.bfloat16)
            k += 1


def finish_call(place, stats, parts):
    rows = parts[0].shape[1]
    width = sum(part.shape[0] for part in parts) * 128
    return pl.pallas_call(
        finish_kernel,
        out_shape=jax.ShapeDtypeStruct((rows, width), jnp.bfloat16),
        in_specs=[SMEM] + [VMEM] * (1 + len(parts)),
        out_specs=VMEM,
        compiler_params=pltpu.CompilerParams(vmem_limit_bytes=16 * 1024 * 1024),
        cost_estimate=pl.CostEstimate(
            flops=2 * rows * width, bytes_accessed=6 * rows * width, transcendentals=0
        ),
    )(place, stats, *parts)


def ring_order(planes):
    return [(z, 0) for z in range(planes)] + [(z, 1) for z in range(planes - 1, -1, -1)]


def pick(index, options):
    out = options[0]
    for k in range(1, len(options)):
        out = jnp.where(index == k, options[k], out)
    return out


def ring_body(planes, gradients, queries, loss_weight):
    order = ring_order(planes)
    nodes = len(order)
    far = nodes // 2
    rows_here, depth = gradients.shape
    feat_size = 2
    feature_count = depth * feat_size
    row_id = lax.axis_index("rows")
    feat = lax.axis_index("feat")
    core = row_id % 2

    def device(node, c):
        z, x = order[node % nodes]
        return (z * 2 + x) * 2 + c

    swap = [(r, r ^ 1) for r in range(2 * nodes)]
    turn = [(device(n, 0), device(n + 1, 0)) for n in range(nodes)]
    turn += [(device(n, 1), device(n - 1, 1)) for n in range(nodes)]

    def hop(value, pairs):
        return lax.ppermute(value, "rows", pairs)

    def cross(value):
        return lax.ppermute(value, "feat", [(0, 1), (1, 0)])

    first, second = [queries], [hop(queries, swap)]
    for s in range(1, far + 1):
        first.append(hop(first[s - 1], turn))
        if s < far:
            second.append(hop(second[s - 1], turn))
    first_other = [None] + [hop(first[s], swap) for s in range(1, far + 1)]
    second_other = [None] + [hop(second[s], swap) for s in range(1, far)]

    shard = queries.shape[0]
    blocks = []
    squares = None
    for s in range(far + 1):
        if s == 0:
            units, places = [first[0], second[0]], [core * shard, shard - core * shard]
        elif s == far:
            units, places = [first[s], first_other[s]], [core * shard, shard - core * shard]
        else:
            units = [first[s], second[s], first_other[s], second_other[s]]
            places = [core * 3, 1 + core, 3 - core * 3, 2 - core]
            places = [p * shard for p in places]
        out = product_call(gradients, units, places, with_squares=s == 0)
        if s == 0:
            out, squares = out
        blocks += [out[b] for b in range(out.shape[0])]
    offsets = [0]
    for s in range(1, far):
        offsets += [-s, s]
    offsets += [far]
    arrival = [0] + [s for s in range(1, far) for _ in range(2)] + [far]

    squares = squares + cross(squares)
    factor = loss_weight[:, None] / jnp.sqrt(squares / feature_count + NORM_EPS)

    half = nodes // 2
    send_table, keep_table, place_table = {}, {}, {}
    for n, (z, x) in enumerate(order):
        for f in range(2):
            mine, other, where = [], [], []
            for j, o in enumerate(offsets):
                oz, ox = order[(n + o) % nodes]
                chip = oz * 2 + ox
                if chip // half == f:
                    mine.append(j)
                    where.append(chip % half)
                else:
                    other.append(j)
            key = (z * 2 + x) * 2 + f
            send_table[key], keep_table[key], place_table[key] = other, mine, where
    key = (row_id // 2) * 2 + feat

    def lookup(table, k):
        return jnp.array([table[i][k] for i in range(2 * nodes)], jnp.int32)[key]

    def choose(table, k):
        used = sorted({table[i][k] for i in range(2 * nodes)})
        index = lookup(table, k)
        out = blocks[used[0]]
        for j in used[1:]:
            out = jnp.where(index == j, blocks[j], out)
        return out

    groups = [[0], [1, 2], [3]] if half == 4 else [[k] for k in range(half)]
    parts, stats = [], []
    for group in groups:
        send = jnp.stack([choose(send_table, k) for k in group])
        keep = jnp.stack([choose(keep_table, k) for k in group])
        scored, stat = score_call(keep, cross(send), factor)
        parts.append(scored)
        stats.append(stat)
    stat = jnp.concatenate(stats, axis=0)
    place = jnp.stack([lookup(place_table, k) for k in range(half)])
    onehot = place[None, :] == jnp.arange(half)[:, None]
    stat = jnp.sum(jnp.where(onehot[:, :, None, None], stat[None], 0.0), axis=1)
    mean = stat[:, 0].reshape(1, half * 128)
    spread = stat[:, 1].reshape(1, half * 128)
    count = rows_here
    step = 1
    while step < 2 * nodes:
        both = jnp.concatenate([mean, spread], axis=0)
        come = hop(both, [(r, r ^ step) for r in range(2 * nodes)])
        gap = come[0:1] - mean
        mean = 0.5 * (mean + come[0:1])
        spread = spread + come[1:2] + (0.5 * count) * (gap * gap)
        count *= 2
        step *= 2
    scale = lax.rsqrt(spread / count + VAR_EPS)
    return finish_call(place, jnp.concatenate([mean, scale], axis=0), parts)


def solution(mesh):
    in_specs = (P("rows", "feat"), P("rows", "feat"), P("rows"))
    out_specs = P("rows", "feat")
    rows, feat = mesh.shape["rows"], mesh.shape["feat"]

    def body(gradients, queries, loss_weight):
        planes = rows // 4
        fits = rows % 4 == 0 and planes & (planes - 1) == 0 and planes >= 2 and feat == 2
        if fits and 2 * queries.shape[0] == 128 and gradients.shape[0] % 256 == 0:
            return ring_body(planes, gradients, queries, loss_weight)
        return plain_body(gradients, queries, loss_weight)

    return jax.shard_map(body, mesh=mesh, in_specs=in_specs, out_specs=out_specs, check_vma=False)
```

```python
import functools

import jax
import jax.numpy as jnp
from jax import lax
from jax.experimental import pallas as pl
from jax.experimental.pallas import tpu as pltpu
from jax.sharding import PartitionSpec as P

NORM_EPS = 1e-06
VAR_EPS = 1e-05
VMEM = pl.BlockSpec(memory_space=pltpu.VMEM)
NT = (((1,), (1,)), ((), ()))


def plain_body(gradients, queries, loss_weight):
    rows_here = gradients.shape[0]
    total_rows = rows_here * lax.axis_size("rows")
    feature_count = gradients.shape[1] * lax.axis_size("feat")
    local_squares = jnp.sum(jnp.square(gradients.astype(jnp.float32)), axis=1)
    squares = lax.psum(local_squares, "feat")
    product = lax.dot_general(
        gradients,
        lax.all_gather(queries, "rows", axis=0, tiled=True),
        NT,
        preferred_element_type=jnp.float32,
    )
    raw = lax.psum_scatter(
        product.astype(jnp.bfloat16), "feat", scatter_dimension=1, tiled=True
    ).astype(jnp.float32)
    factor = loss_weight / jnp.sqrt(squares / feature_count + NORM_EPS)
    scored = raw * factor[:, None]
    column_mean = lax.psum(jnp.sum(scored, axis=0), "rows") / total_rows
    centered = scored - column_mean[None, :]
    square_sums = lax.psum(jnp.sum(centered * centered, axis=0), "rows")
    column_var = square_sums / total_rows
    return (centered * lax.rsqrt(column_var + VAR_EPS)[None, :]).astype(jnp.bfloat16)


def ring_order(planes):
    return [(z, 0) for z in range(planes)] + [(z, 1) for z in range(planes - 1, -1, -1)]


class Plan:
    def __init__(self, planes):
        self.planes = planes
        self.order = ring_order(planes)
        self.nodes = len(self.order)
        self.far = self.nodes // 2
        low, high = [0], [0]
        for s in range(1, self.far):
            low += [-s, s]
            high += [s, -s]
        self.offsets = (low + [self.far], high + [self.far])
        self.pairs = len(self.offsets[0])
        self.turns = self.pairs // 2
        self.give, self.take, self.place = {}, {}, {}
        for n, (z, x) in enumerate(self.order):
            for f in range(2):
                key = (z * 2 + x) * 2 + f
                for half in range(2):
                    mine, other = [], []
                    spot = [0] * self.turns
                    for p, o in enumerate(self.offsets[half]):
                        oz, ox = self.order[(n + o) % self.nodes]
                        chip = oz * 2 + ox
                        if chip // self.turns == f:
                            spot[chip % self.turns] = len(mine)
                            mine.append(p)
                        else:
                            other.append(p)
                    self.give[key, half] = other
                    self.take[key, half] = mine
                    self.place[key, half] = spot

    def packed(self, table, half):
        key = (lax.axis_index("rows") // 2) * 2 + lax.axis_index("feat")
        codes = [sum(v << (4 * m) for m, v in enumerate(table[k, half])) for k in range(2 * self.nodes)]
        code = jnp.int32(codes[0])
        for k in range(1, 2 * self.nodes):
            code = jnp.where(key == k, jnp.int32(codes[k]), code)
        return code

    def options(self, table, half, m):
        return sorted({table[k, half][m] for k in range(2 * self.nodes)})


def entry(code, m):
    return (code >> (4 * m)) & 15


def gather_block(plan, table, m, blocks, held):
    for half in range(2):
        index = entry(plan.packed(table, half), m)
        for p in plan.options(table, half, m):
            @pl.when(index == p)
            def _(half=half, p=p):
                held[half] = blocks[p]()
    lane = lax.broadcasted_iota(jnp.int32, held.shape[1:], 1)
    return jnp.where(lane < held.shape[2] // 2, held[0], held[1])


def product_kernel(plan, sources, count, turn, known, grad_ref, *refs):
    units, refs = refs[:count], refs[count:]
    older, refs = refs[:len(known)], refs[len(known):]
    out_ref, refs = refs[0], refs[1:]
    if turn is not None:
        send_ref, held, pick = refs
    else:
        (held,) = refs
    shard = units[0].shape[0]
    core = lax.axis_index("rows") % 2
    for k in range(count):
        pair, same = k // 2, sources[k]
        spot = pair * 2 + (core if same else 1 - core)
        held[pl.ds(pl.multiple_of(spot * shard, shard), shard), :] = units[k][...]
    product = lax.dot_general(grad_ref[...], held[...], NT, preferred_element_type=jnp.float32)
    for b in range(out_ref.shape[0]):
        out_ref[b] = product[:, b * 128:(b + 1) * 128].astype(jnp.bfloat16)
    if turn is not None:
        blocks = block_readers(known, older)
        first = sum(n for n, _ in known) if known else 0
        for b in range(out_ref.shape[0]):
            blocks[first + b] = lambda b=b: out_ref[b]
        send_ref[...] = gather_block(plan, plan.give, turn, blocks, pick)


def block_readers(known, refs):
    blocks, p = {}, 0
    for (n, _), ref in zip(known, refs):
        for b in range(n):
            blocks[p] = lambda ref=ref, b=b: ref[b]
            p += 1
    return blocks


def product_call(plan, gradients, units, sources, known=(), turn=None):
    rows, depth = gradients.shape
    shard = units[0].shape[0]
    count = len(units)
    n = count // 2
    out_shape = [jax.ShapeDtypeStruct((n, rows, 128), jnp.bfloat16)]
    scratch = [pltpu.VMEM((count * shard, depth), jnp.bfloat16)]
    if turn is None:
        known = ()
    else:
        out_shape.append(jax.ShapeDtypeStruct((rows, 128), jnp.bfloat16))
        scratch.append(pltpu.VMEM((2, rows, 128), jnp.bfloat16))
    known = list(known)
    return pl.pallas_call(
        functools.partial(product_kernel, plan, sources, count, turn, known),
        out_shape=out_shape,
        in_specs=[VMEM] * (1 + count + len(known)),
        out_specs=[VMEM] * len(out_shape),
        scratch_shapes=scratch,
        compiler_params=pltpu.CompilerParams(vmem_limit_bytes=20 * 1024 * 1024),
        cost_estimate=pl.CostEstimate(
            flops=2 * rows * depth * count * shard, bytes_accessed=2 * rows * depth, transcendentals=0
        ),
    )(gradients, *units, *[a for _, a in known])


def squares_kernel(grad_ref, out_ref):
    def step(i, carry):
        rows = pl.ds(pl.multiple_of(i * 64, 64), 64)
        total = jnp.zeros((64, 128), jnp.float32)
        for k in range(grad_ref.shape[1] // 128):
            wide = grad_ref[rows, k * 128:(k + 1) * 128].astype(jnp.float32)
            total = total + wide * wide
        out_ref[rows, :] = jnp.sum(total, axis=1, keepdims=True)
        return carry

    lax.fori_loop(0, grad_ref.shape[0] // 64, step, 0)


def squares_call(gradients):
    rows, depth = gradients.shape
    return pl.pallas_call(
        squares_kernel,
        out_shape=jax.ShapeDtypeStruct((rows, 1), jnp.float32),
        in_specs=[VMEM],
        out_specs=VMEM,
        compiler_params=pltpu.CompilerParams(vmem_limit_bytes=16 * 1024 * 1024),
        cost_estimate=pl.CostEstimate(flops=2 * rows * depth, bytes_accessed=2 * rows * depth, transcendentals=0),
    )(gradients)


def score_kernel(plan, turns, known, last, *refs):
    comes, refs = refs[:len(turns)], refs[len(turns):]
    factor_ref, refs = refs[0], refs[1:]
    older, refs = refs[:len(known)], refs[len(known):]
    if last:
        before_ref, scored_ref, stat_ref, pick = refs
    else:
        scored_ref, stat_ref, pick = refs
    blocks = block_readers(known, older)
    stats = []
    for b, turn in enumerate(turns):
        keep = gather_block(plan, plan.take, turn, blocks, pick)
        raw = keep.astype(jnp.float32) + comes[b][...].astype(jnp.float32)
        scored = raw * factor_ref[...]
        scored_ref[b] = scored
        mean = jnp.sum(scored, axis=0, keepdims=True) / scored.shape[0]
        centered = scored - mean
        both = jnp.concatenate([mean, jnp.sum(centered * centered, axis=0, keepdims=True)], axis=0)
        if last:
            stats.append(both)
        else:
            stat_ref[b] = both
    if last:
        stats = [before_ref[b] for b in range(before_ref.shape[0])] + stats
        lane = lax.broadcasted_iota(jnp.int32, (2, 128), 1)
        codes = [plan.packed(plan.place, half) for half in range(2)]
        for j in range(plan.turns):
            halves = []
            for half in range(2):
                index = entry(codes[half], j)
                value = stats[0]
                for m in range(1, len(stats)):
                    value = jnp.where(index == m, stats[m], value)
                halves.append(value)
            stat_ref[:, j * 128:(j + 1) * 128] = jnp.where(lane < 64, halves[0], halves[1])


def score_call(plan, turns, comes, factor, known, before=None):
    rows = factor.shape[0]
    last = before is not None
    n = len(turns)
    stat = (2, plan.turns * 128) if last else (n, 2, 128)
    args = list(comes) + [factor] + [a for _, a in known] + ([before] if last else [])
    return pl.pallas_call(
        functools.partial(score_kernel, plan, turns, known, last),
        out_shape=[jax.ShapeDtypeStruct((n, rows, 128), jnp.float32), jax.ShapeDtypeStruct(stat, jnp.float32)],
        in_specs=[VMEM] * len(args),
        out_specs=[VMEM] * 2,
        scratch_shapes=[pltpu.VMEM((2, rows, 128), jnp.bfloat16)],
        compiler_params=pltpu.CompilerParams(vmem_limit_bytes=16 * 1024 * 1024),
        cost_estimate=pl.CostEstimate(flops=8 * n * rows * 128, bytes_accessed=12 * n * rows * 128, transcendentals=0),
    )(*args)


def finish_kernel(plan, count, stat_ref, early_ref, late_ref, out_ref):
    lane = lax.broadcasted_iota(jnp.int32, late_ref.shape[1:], 1)
    codes = [plan.packed(plan.place, half) for half in range(2)]
    early = early_ref.shape[0]
    scale = lax.rsqrt(stat_ref[1:2, :] / count + VAR_EPS)
    for j in range(plan.turns):
        halves = []
        for half in range(2):
            index = entry(codes[half], j)
            value = early_ref[jnp.minimum(index, early - 1)]
            halves.append(jnp.where(index < early, value, late_ref[0]))
        value = jnp.where(lane < 64, halves[0], halves[1])
        columns = slice(j * 128, (j + 1) * 128)
        out_ref[:, columns] = ((value - stat_ref[0:1, columns]) * scale[:, columns]).astype(jnp.bfloat16)


def finish_call(plan, count, stat, early, late):
    rows = late.shape[1]
    width = plan.turns * 128
    return pl.pallas_call(
        functools.partial(finish_kernel, plan, count),
        out_shape=jax.ShapeDtypeStruct((rows, width), jnp.bfloat16),
        in_specs=[VMEM] * 3,
        out_specs=VMEM,
        compiler_params=pltpu.CompilerParams(vmem_limit_bytes=16 * 1024 * 1024),
        cost_estimate=pl.CostEstimate(flops=2 * rows * width, bytes_accessed=6 * rows * width, transcendentals=0),
    )(stat, early, late)


def ring_body(planes, gradients, queries, loss_weight):
    plan = Plan(planes)
    nodes, far = plan.nodes, plan.far
    rows_here, depth = gradients.shape
    feature_count = depth * 2

    def device(node, c):
        z, x = plan.order[node % nodes]
        return (z * 2 + x) * 2 + c

    swap = [(r, r ^ 1) for r in range(2 * nodes)]
    turn = [(device(n, 0), device(n + 1, 0)) for n in range(nodes)]
    turn += [(device(n, 1), device(n - 1, 1)) for n in range(nodes)]

    def hop(value, pairs):
        return lax.ppermute(value, "rows", pairs)

    def cross(value):
        return lax.ppermute(value, "feat", [(0, 1), (1, 0)])

    first, second = [queries], [hop(queries, swap)]
    for s in range(1, far + 1):
        first.append(hop(first[s - 1], turn))
        if s < far:
            second.append(hop(second[s - 1], turn))
    arrived = [([queries, second[0]], [True, False])]
    for s in range(1, far + 1):
        arrived.append(([first[s], hop(first[s], swap)], [True, False]))
        if s < far:
            arrived.append(([second[s], hop(second[s], swap)], [False, True]))

    squares = squares_call(gradients)
    squares = squares + cross(squares)
    factor = loss_weight[:, None] / jnp.sqrt(squares / feature_count + NORM_EPS)

    known, comes = [], []
    p = 0
    while p < plan.pairs:
        m = len(comes)
        ready = max(max(plan.options(plan.give, half, m)) for half in range(2))
        n = 2 if p + 1 < ready and p + 1 < plan.pairs else 1
        units, sources = [], []
        for u, s in arrived[p:p + n]:
            units, sources = units + u, sources + s
        done = p + n > ready
        out = product_call(plan, gradients, units, sources, known, m if done else None)
        known.append((n, out[0]))
        if done:
            comes.append(cross(out[1]))
        p += n
    last = len(comes) - 1
    early, stat = score_call(plan, list(range(last)), comes[:last], factor, known)
    late, stat = score_call(plan, [last], comes[last:], factor, known, stat)

    mean, spread = stat[0:1], stat[1:2]
    count, step = rows_here, 1
    while step < 2 * nodes:
        come = hop(jnp.concatenate([mean, spread], axis=0), [(r, r ^ step) for r in range(2 * nodes)])
        gap = come[0:1] - mean
        mean = 0.5 * (mean + come[0:1])
        spread = spread + come[1:2] + (0.5 * count) * (gap * gap)
        count *= 2
        step *= 2
    return finish_call(plan, count, jnp.concatenate([mean, spread], axis=0), early, late)


def solution(mesh):
    in_specs = (P("rows", "feat"), P("rows", "feat"), P("rows"))
    out_specs = P("rows", "feat")
    rows, feat = mesh.shape["rows"], mesh.shape["feat"]

    def body(gradients, queries, loss_weight):
        planes = rows // 4
        fits = rows % 4 == 0 and planes & (planes - 1) == 0 and planes >= 2 and feat == 2
        if fits and 2 * queries.shape[0] == 128 and gradients.shape[0] % 256 == 0:
            return ring_body(planes, gradients, queries, loss_weight)
        return plain_body(gradients, queries, loss_weight)

    return jax.shard_map(body, mesh=mesh, in_specs=in_specs, out_specs=out_specs, check_vma=False)
```

```python
import functools

import jax
import jax.numpy as jnp
from jax import lax
from jax.experimental import pallas as pl
from jax.experimental.pallas import tpu as pltpu
from jax.sharding import PartitionSpec as P


NORM_EPS = 1e-06
VAR_EPS = 1e-05
VMEM = pl.BlockSpec(memory_space=pltpu.VMEM)
NT = (((1,), (1,)), ((), ()))


def plain_body(gradients, queries, loss_weight):
    rows_here = gradients.shape[0]
    total_rows = rows_here * lax.axis_size("rows")
    feature_count = gradients.shape[1] * lax.axis_size("feat")
    local_squares = jnp.sum(jnp.square(gradients.astype(jnp.float32)), axis=1)
    squares = lax.psum(local_squares, "feat")
    product = lax.dot_general(
        gradients,
        lax.all_gather(queries, "rows", axis=0, tiled=True),
        NT,
        preferred_element_type=jnp.float32,
    )
    raw = lax.psum_scatter(
        product.astype(jnp.bfloat16), "feat", scatter_dimension=1, tiled=True
    ).astype(jnp.float32)
    factor = loss_weight / jnp.sqrt(squares / feature_count + NORM_EPS)
    scored = raw * factor[:, None]
    column_mean = lax.psum(jnp.sum(scored, axis=0), "rows") / total_rows
    centered = scored - column_mean[None, :]
    square_sums = lax.psum(jnp.sum(centered * centered, axis=0), "rows")
    column_var = square_sums / total_rows
    return (centered * lax.rsqrt(column_var + VAR_EPS)[None, :]).astype(jnp.bfloat16)


def ring_order(planes):
    return [(z, 0) for z in range(planes)] + [(z, 1) for z in range(planes - 1, -1, -1)]


class Plan:
    def __init__(self, planes):
        self.order = ring_order(planes)
        self.nodes = len(self.order)
        self.far = self.nodes // 2
        low, high = [0], [0]
        for s in range(1, self.far):
            low += [-s, s]
            high += [s, -s]
        self.offsets = (low + [self.far], high + [self.far])
        self.pairs = len(self.offsets[0])
        self.turns = self.pairs // 2
        self.give, self.take, self.place = {}, {}, {}
        for n, (z, x) in enumerate(self.order):
            for f in range(2):
                key = (z * 2 + x) * 2 + f
                for half in range(2):
                    mine, other = [], []
                    spot = [0] * self.turns
                    for p, o in enumerate(self.offsets[half]):
                        oz, ox = self.order[(n + o) % self.nodes]
                        chip = oz * 2 + ox
                        if chip // self.turns == f:
                            spot[chip % self.turns] = len(mine)
                            mine.append(p)
                        else:
                            other.append(p)
                    self.give[key, half] = other
                    self.take[key, half] = mine
                    self.place[key, half] = spot

    def packed(self, table, half):
        key = (lax.axis_index("rows") // 2) * 2 + lax.axis_index("feat")
        codes = [sum(v << (4 * m) for m, v in enumerate(table[k, half])) for k in range(2 * self.nodes)]
        code = jnp.int32(codes[0])
        for k in range(1, 2 * self.nodes):
            code = jnp.where(key == k, jnp.int32(codes[k]), code)
        return code

    def options(self, table, half, m):
        return sorted({table[k, half][m] for k in range(2 * self.nodes)})


def entry(code, m):
    return (code >> (4 * m)) & 15


def gather_block(plan, table, m, blocks, held):
    for half in range(2):
        index = entry(plan.packed(table, half), m)
        for p in plan.options(table, half, m):
            @pl.when(index == p)
            def _(half=half, p=p):
                held[half] = blocks[p]()
    lane = lax.broadcasted_iota(jnp.int32, held.shape[1:], 1)
    return jnp.where(lane < held.shape[2] // 2, held[0], held[1])


def product_kernel(plan, sources, count, turn, known, grad_ref, *refs):
    units, refs = refs[:count], refs[count:]
    older, refs = refs[:len(known)], refs[len(known):]
    out_ref, refs = refs[0], refs[2:]
    if turn is not None:
        send_ref, held, pick = refs
    else:
        (held,) = refs
    shard = units[0].shape[0]
    core = lax.axis_index("rows") % 2
    for k in range(count):
        pair, same = k // 2, sources[k]
        spot = pair * 2 + (core if same else 1 - core)
        held[pl.ds(pl.multiple_of(spot * shard, shard), shard), :] = units[k][...]
    product = lax.dot_general(grad_ref[...], held[...], NT, preferred_element_type=jnp.float32)
    for b in range(out_ref.shape[0]):
        out_ref[b] = product[:, b * 128:(b + 1) * 128].astype(jnp.bfloat16)
    if turn is not None:
        blocks = block_readers(known, older)
        first = sum(n for n, _ in known) if known else 0
        for b in range(out_ref.shape[0]):
            blocks[first + b] = lambda b=b: out_ref[b]
        send_ref[...] = gather_block(plan, plan.give, turn, blocks, pick)


def block_readers(known, refs):
    blocks, p = {}, 0
    for (n, _), ref in zip(known, refs):
        for b in range(n):
            blocks[p] = lambda ref=ref, b=b: ref[b]
            p += 1
    return blocks


def product_call(plan, gradients, units, sources, known=(), turn=None):
    rows, depth = gradients.shape
    shard = units[0].shape[0]
    count = len(units)
    n = count // 2
    out_shape = [
        jax.ShapeDtypeStruct((n, rows, 128), jnp.bfloat16),
        jax.ShapeDtypeStruct(gradients.shape, gradients.dtype),
    ]
    scratch = [pltpu.VMEM((count * shard, depth), jnp.bfloat16)]
    if turn is None:
        known = ()
    else:
        out_shape.append(jax.ShapeDtypeStruct((rows, 128), jnp.bfloat16))
        scratch.append(pltpu.VMEM((2, rows, 128), jnp.bfloat16))
    known = list(known)
    return pl.pallas_call(
        functools.partial(product_kernel, plan, sources, count, turn, known),
        out_shape=out_shape,
        in_specs=[VMEM] * (1 + count + len(known)),
        out_specs=[VMEM] * len(out_shape),
        scratch_shapes=scratch,
        input_output_aliases={0: 1},
        compiler_params=pltpu.CompilerParams(vmem_limit_bytes=12 * 1024 * 1024),
        cost_estimate=pl.CostEstimate(
            flops=2 * rows * depth * count * shard, bytes_accessed=2 * rows * depth, transcendentals=0
        ),
    )(gradients, *units, *[a for _, a in known])


def load_kernel(parts, grad_ref, held_ref, square_ref, sem):
    rows, depth = held_ref.shape
    piece = rows // parts
    copies = [
        pltpu.make_async_copy(grad_ref.at[pl.ds(k * piece, piece)], held_ref.at[pl.ds(k * piece, piece)], sem.at[k])
        for k in range(parts)
    ]
    for copy in copies:
        copy.start()
    for k, copy in enumerate(copies):
        copy.wait()

        def step(i, carry, k=k):
            here = pl.ds(pl.multiple_of(k * piece + i * 64, 64), 64)
            total = jnp.zeros((64, 128), jnp.float32)
            for c in range(depth // 128):
                wide = held_ref[here, c * 128:(c + 1) * 128].astype(jnp.float32)
                total = total + wide * wide
            square_ref[here, :] = jnp.sum(total, axis=1, keepdims=True)
            return carry

        lax.fori_loop(0, piece // 64, step, 0)


def load_call(gradients, parts=4):
    rows, depth = gradients.shape
    return pl.pallas_call(
        functools.partial(load_kernel, parts),
        out_shape=[
            jax.ShapeDtypeStruct((rows, depth), gradients.dtype),
            jax.ShapeDtypeStruct((rows, 1), jnp.float32),
        ],
        in_specs=[pl.BlockSpec(memory_space=pltpu.HBM)],
        out_specs=[VMEM, VMEM],
        scratch_shapes=[pltpu.SemaphoreType.DMA((parts,))],
        compiler_params=pltpu.CompilerParams(vmem_limit_bytes=8 * 1024 * 1024),
        cost_estimate=pl.CostEstimate(flops=2 * rows * depth, bytes_accessed=2 * rows * depth, transcendentals=0),
    )(pltpu.with_memory_space_constraint(gradients, pltpu.HBM))


def score_kernel(plan, turns, known, first, depth, *refs):
    comes, refs = refs[:len(turns)], refs[len(turns):]
    if first:
        square_ref, other_ref, weight_ref, refs = *refs[:3], refs[3:]
    else:
        factor_ref, before_ref, refs = *refs[:2], refs[2:]
    older, refs = refs[:len(known)], refs[len(known):]
    if first:
        scored_ref, stat_ref, factor_ref, pick = refs
        eye = lax.broadcasted_iota(jnp.int32, (128, 128), 0) == lax.broadcasted_iota(jnp.int32, (128, 128), 1)
        for i in range(weight_ref.shape[0]):
            rows = slice(i * 128, (i + 1) * 128)
            weight = jnp.sum(jnp.where(eye, weight_ref[i:i + 1, :], 0.0), axis=1, keepdims=True)
            squares = square_ref[rows, :] + other_ref[rows, :]
            factor_ref[rows, :] = weight / jnp.sqrt(squares / depth + NORM_EPS)
    else:
        scored_ref, stat_ref, pick = refs
    blocks = block_readers(known, older)
    stats = []
    for b, turn in enumerate(turns):
        keep = gather_block(plan, plan.take, turn, blocks, pick)
        raw = keep.astype(jnp.float32) + comes[b][...].astype(jnp.float32)
        scored = raw * factor_ref[...]
        scored_ref[b] = scored
        mean = jnp.sum(scored, axis=0, keepdims=True) / scored.shape[0]
        centered = scored - mean
        both = jnp.concatenate([mean, jnp.sum(centered * centered, axis=0, keepdims=True)], axis=0)
        if first:
            stat_ref[b] = both
        else:
            stats.append(both)
    if not first:
        stats = [before_ref[b] for b in range(before_ref.shape[0])] + stats
        lane = lax.broadcasted_iota(jnp.int32, (2, 128), 1)
        codes = [plan.packed(plan.place, half) for half in range(2)]
        for j in range(plan.turns):
            halves = []
            for half in range(2):
                index = entry(codes[half], j)
                value = stats[0]
                for m in range(1, len(stats)):
                    value = jnp.where(index == m, stats[m], value)
                halves.append(value)
            stat_ref[:, j * 128:(j + 1) * 128] = jnp.where(lane < 64, halves[0], halves[1])


def score_call(plan, turns, comes, known, depth, squares=None, factor=None, before=None):
    rows = comes[0].shape[0]
    first = squares is not None
    n = len(turns)
    stat = (n, 2, 128) if first else (2, plan.turns * 128)
    args = list(comes) + (list(squares) if first else [factor, before]) + [a for _, a in known]
    out_shape = [jax.ShapeDtypeStruct((n, rows, 128), jnp.float32), jax.ShapeDtypeStruct(stat, jnp.float32)]
    if first:
        out_shape.append(jax.ShapeDtypeStruct((rows, 1), jnp.float32))
    return pl.pallas_call(
        functools.partial(score_kernel, plan, turns, known, first, depth),
        out_shape=out_shape,
        in_specs=[VMEM] * len(args),
        out_specs=[VMEM] * len(out_shape),
        scratch_shapes=[pltpu.VMEM((2, rows, 128), jnp.bfloat16)],
        compiler_params=pltpu.CompilerParams(vmem_limit_bytes=8 * 1024 * 1024),
        cost_estimate=pl.CostEstimate(flops=8 * n * rows * 128, bytes_accessed=12 * n * rows * 128, transcendentals=0),
    )(*args)


def finish_kernel(plan, count, stat_ref, early_ref, late_ref, out_ref):
    lane = lax.broadcasted_iota(jnp.int32, late_ref.shape[1:], 1)
    codes = [plan.packed(plan.place, half) for half in range(2)]
    early = early_ref.shape[0]
    scale = lax.rsqrt(stat_ref[1:2, :] / count + VAR_EPS)
    for j in range(plan.turns):
        halves = []
        for half in range(2):
            index = entry(codes[half], j)
            value = early_ref[jnp.minimum(index, early - 1)]
            halves.append(jnp.where(index < early, value, late_ref[0]))
        value = jnp.where(lane < 64, halves[0], halves[1])
        columns = slice(j * 128, (j + 1) * 128)
        out_ref[:, columns] = ((value - stat_ref[0:1, columns]) * scale[:, columns]).astype(jnp.bfloat16)


def finish_call(plan, count, stat, early, late):
    rows = late.shape[1]
    width = plan.turns * 128
    return pl.pallas_call(
        functools.partial(finish_kernel, plan, count),
        out_shape=jax.ShapeDtypeStruct((rows, width), jnp.bfloat16),
        in_specs=[VMEM] * 3,
        out_specs=VMEM,
        compiler_params=pltpu.CompilerParams(vmem_limit_bytes=8 * 1024 * 1024),
        cost_estimate=pl.CostEstimate(flops=2 * rows * width, bytes_accessed=6 * rows * width, transcendentals=0),
    )(stat, early, late)


def product_groups(plan):
    groups, p, m = [], 0, 0
    while p < plan.pairs:
        ready = max(max(plan.options(plan.give, half, m)) for half in range(2))
        n = 2 if p + 1 < ready and p + 1 < plan.pairs else 1
        done = p + n > ready
        groups.append((p, n, m if done else None))
        m += done
        p += n
    return groups


def ring_body(planes, gradients, queries, loss_weight):
    plan = Plan(planes)
    nodes, far = plan.nodes, plan.far
    rows_here, depth = gradients.shape
    feature_count = depth * 2

    def device(node, c):
        z, x = plan.order[node % nodes]
        return (z * 2 + x) * 2 + c

    swap = [(r, r ^ 1) for r in range(2 * nodes)]
    turn = [(device(n, 0), device(n + 1, 0)) for n in range(nodes)]
    turn += [(device(n, 1), device(n - 1, 1)) for n in range(nodes)]

    def cross(value):
        return lax.ppermute(value, "feat", [(0, 1), (1, 0)])

    ring = [queries, lax.ppermute(queries, "rows", swap)]
    for _ in range(1, 2 * far):
        ring.append(lax.ppermute(ring[-2], "rows", turn))
    arrived = [([queries, ring[1]], [True, False])]
    for k in range(1, 2 * far):
        arrived.append(([ring[k + 1], lax.ppermute(ring[k + 1], "rows", swap)], [k % 2 == 1, k % 2 == 0]))

    gradients, squares = load_call(gradients)
    squares = (squares, cross(squares), loss_weight.reshape(rows_here // 128, 128))

    known, comes = [], []
    for p, n, m in product_groups(plan):
        units, sources = [], []
        for u, s in arrived[p:p + n]:
            units, sources = units + u, sources + s
        out = product_call(plan, gradients, units, sources, known, m)
        known.append((n, out[0]))
        if m is not None:
            comes.append(cross(out[2]))
        gradients = out[1]
    last = len(comes) - 1
    early, stat, factor = score_call(plan, list(range(last)), comes[:last], known, feature_count, squares)
    late, stat = score_call(plan, [last], comes[last:], known, feature_count, None, factor, stat)

    mean, spread = stat[0:1], stat[1:2]
    count, step = rows_here, 1
    while step < 2 * nodes:
        pairs = [(r, r ^ step) for r in range(2 * nodes)]
        come = lax.ppermute(jnp.concatenate([mean, spread], axis=0), "rows", pairs)
        gap = come[0:1] - mean
        mean = 0.5 * (mean + come[0:1])
        spread = spread + come[1:2] + (0.5 * count) * (gap * gap)
        count *= 2
        step *= 2
    return finish_call(plan, count, jnp.concatenate([mean, spread], axis=0), early, late)


def solution(mesh):
    in_specs = (P("rows", "feat"), P("rows", "feat"), P("rows"))
    out_specs = P("rows", "feat")
    rows, feat = mesh.shape["rows"], mesh.shape["feat"]
    planes = rows // 4
    fits = rows == 4 * planes and planes in (2, 4) and feat == 2

    def body(gradients, queries, loss_weight):
        if fits and 2 * queries.shape[0] == 128 and gradients.shape[0] % 256 == 0:
            return ring_body(planes, gradients, queries, loss_weight)
        return plain_body(gradients, queries, loss_weight)

    return jax.shard_map(body, mesh=mesh, in_specs=in_specs, out_specs=out_specs, check_vma=False)
```

```python
import functools

import jax
import jax.numpy as jnp
from jax import lax
from jax.experimental import pallas as pl
from jax.experimental.pallas import tpu as pltpu
from jax.sharding import PartitionSpec as P


NORM_EPS = 1e-06
VAR_EPS = 1e-05
VMEM = pl.BlockSpec(memory_space=pltpu.VMEM)
NT = (((1,), (1,)), ((), ()))


def plain_body(gradients, queries, loss_weight):
    rows_here = gradients.shape[0]
    total_rows = rows_here * lax.axis_size("rows")
    feature_count = gradients.shape[1] * lax.axis_size("feat")
    local_squares = jnp.sum(jnp.square(gradients.astype(jnp.float32)), axis=1)
    squares = lax.psum(local_squares, "feat")
    product = lax.dot_general(
        gradients,
        lax.all_gather(queries, "rows", axis=0, tiled=True),
        NT,
        preferred_element_type=jnp.float32,
    )
    raw = lax.psum_scatter(
        product.astype(jnp.bfloat16), "feat", scatter_dimension=1, tiled=True
    ).astype(jnp.float32)
    factor = loss_weight / jnp.sqrt(squares / feature_count + NORM_EPS)
    scored = raw * factor[:, None]
    column_mean = lax.psum(jnp.sum(scored, axis=0), "rows") / total_rows
    centered = scored - column_mean[None, :]
    square_sums = lax.psum(jnp.sum(centered * centered, axis=0), "rows")
    column_var = square_sums / total_rows
    return (centered * lax.rsqrt(column_var + VAR_EPS)[None, :]).astype(jnp.bfloat16)


def ring_order(planes):
    return [(z, 0) for z in range(planes)] + [(z, 1) for z in range(planes - 1, -1, -1)]


class Plan:
    def __init__(self, planes):
        self.order = ring_order(planes)
        self.nodes = len(self.order)
        self.far = self.nodes // 2
        low, high = [0], [0]
        for s in range(1, self.far):
            low += [-s, s]
            high += [s, -s]
        self.offsets = (low + [self.far], high + [self.far])
        self.pairs = len(self.offsets[0])
        self.turns = self.pairs // 2
        self.give, self.take, self.place = {}, {}, {}
        for n, (z, x) in enumerate(self.order):
            for f in range(2):
                key = (z * 2 + x) * 2 + f
                for half in range(2):
                    mine, other = [], []
                    spot = [0] * self.turns
                    for p, o in enumerate(self.offsets[half]):
                        oz, ox = self.order[(n + o) % self.nodes]
                        chip = oz * 2 + ox
                        if chip // self.turns == f:
                            spot[chip % self.turns] = len(mine)
                            mine.append(p)
                        else:
                            other.append(p)
                    self.give[key, half] = other
                    self.take[key, half] = mine
                    self.place[key, half] = spot

    def packed(self, table, half):
        key = (lax.axis_index("rows") // 2) * 2 + lax.axis_index("feat")
        codes = [sum(v << (4 * m) for m, v in enumerate(table[k, half])) for k in range(2 * self.nodes)]
        code = jnp.int32(codes[0])
        for k in range(1, 2 * self.nodes):
            code = jnp.where(key == k, jnp.int32(codes[k]), code)
        return code

    def options(self, table, half, m):
        return sorted({table[k, half][m] for k in range(2 * self.nodes)})


def entry(code, m):
    return (code >> (4 * m)) & 15


def gather_block(plan, table, m, blocks, held):
    for half in range(2):
        index = entry(plan.packed(table, half), m)
        for p in plan.options(table, half, m):
            @pl.when(index == p)
            def _(half=half, p=p):
                held[half] = blocks[p]()
    lane = lax.broadcasted_iota(jnp.int32, held.shape[1:], 1)
    return jnp.where(lane < held.shape[2] // 2, held[0], held[1])


def product_kernel(plan, sources, count, turn, known, grad_ref, *refs):
    units, refs = refs[:count], refs[count:]
    older, refs = refs[:len(known)], refs[len(known):]
    out_ref, refs = refs[0], refs[2:]
    if turn is not None:
        send_ref, held, pick = refs
    else:
        (held,) = refs
    shard = units[0].shape[0]
    core = lax.axis_index("rows") % 2
    for k in range(count):
        pair, same = k // 2, sources[k]
        spot = pair * 2 + (core if same else 1 - core)
        held[pl.ds(pl.multiple_of(spot * shard, shard), shard), :] = units[k][...]
    product = lax.dot_general(grad_ref[...], held[...], NT, preferred_element_type=jnp.float32)
    for b in range(out_ref.shape[0]):
        out_ref[b] = product[:, b * 128:(b + 1) * 128].astype(jnp.bfloat16)
    if turn is not None:
        blocks = block_readers(known, older)
        first = sum(n for n, _ in known) if known else 0
        for b in range(out_ref.shape[0]):
            blocks[first + b] = lambda b=b: out_ref[b]
        send_ref[...] = gather_block(plan, plan.give, turn, blocks, pick)


def block_readers(known, refs):
    blocks, p = {}, 0
    for (n, _), ref in zip(known, refs):
        for b in range(n):
            blocks[p] = lambda ref=ref, b=b: ref[b]
            p += 1
    return blocks


def product_call(plan, gradients, units, sources, known=(), turn=None):
    rows, depth = gradients.shape
    shard = units[0].shape[0]
    count = len(units)
    n = count // 2
    out_shape = [
        jax.ShapeDtypeStruct((n, rows, 128), jnp.bfloat16),
        jax.ShapeDtypeStruct(gradients.shape, gradients.dtype),
    ]
    scratch = [pltpu.VMEM((count * shard, depth), jnp.bfloat16)]
    if turn is None:
        known = ()
    else:
        out_shape.append(jax.ShapeDtypeStruct((rows, 128), jnp.bfloat16))
        scratch.append(pltpu.VMEM((2, rows, 128), jnp.bfloat16))
    known = list(known)
    return pl.pallas_call(
        functools.partial(product_kernel, plan, sources, count, turn, known),
        out_shape=out_shape,
        in_specs=[VMEM] * (1 + count + len(known)),
        out_specs=[VMEM] * len(out_shape),
        scratch_shapes=scratch,
        input_output_aliases={0: 1},
        compiler_params=pltpu.CompilerParams(vmem_limit_bytes=12 * 1024 * 1024),
        cost_estimate=pl.CostEstimate(
            flops=2 * rows * depth * count * shard, bytes_accessed=2 * rows * depth, transcendentals=0
        ),
    )(gradients, *units, *[a for _, a in known])


def diagonal():
    return lax.broadcasted_iota(jnp.int32, (128, 128), 0) == lax.broadcasted_iota(jnp.int32, (128, 128), 1)


def load_kernel(parts, grad_ref, held_ref, square_ref, sums_ref, sem):
    rows, depth = held_ref.shape
    piece = rows // parts
    copies = [
        pltpu.make_async_copy(grad_ref.at[pl.ds(k * piece, piece)], held_ref.at[pl.ds(k * piece, piece)], sem.at[k])
        for k in range(parts)
    ]
    for copy in copies:
        copy.start()
    for k, copy in enumerate(copies):
        copy.wait()

        def step(i, carry, k=k):
            here = pl.ds(pl.multiple_of(k * piece + i * 64, 64), 64)
            total = jnp.zeros((64, 128), jnp.float32)
            for c in range(depth // 128):
                wide = held_ref[here, c * 128:(c + 1) * 128].astype(jnp.float32)
                total = total + wide * wide
            sums_ref[here, :] = jnp.sum(total, axis=1, keepdims=True)
            return carry

        lax.fori_loop(0, piece // 64, step, 0)
    for i in range(square_ref.shape[0]):
        column = sums_ref[i * 128:(i + 1) * 128, :]
        square_ref[i:i + 1, :] = jnp.sum(jnp.where(diagonal(), column, 0.0), axis=0, keepdims=True)


def load_call(gradients, parts=4):
    rows, depth = gradients.shape
    return pl.pallas_call(
        functools.partial(load_kernel, parts),
        out_shape=[
            jax.ShapeDtypeStruct((rows, depth), gradients.dtype),
            jax.ShapeDtypeStruct((rows // 128, 128), jnp.float32),
        ],
        in_specs=[pl.BlockSpec(memory_space=pltpu.HBM)],
        out_specs=[VMEM, VMEM],
        scratch_shapes=[pltpu.VMEM((rows, 1), jnp.float32), pltpu.SemaphoreType.DMA((parts,))],
        compiler_params=pltpu.CompilerParams(vmem_limit_bytes=8 * 1024 * 1024),
        cost_estimate=pl.CostEstimate(flops=2 * rows * depth, bytes_accessed=2 * rows * depth, transcendentals=0),
    )(pltpu.with_memory_space_constraint(gradients, pltpu.HBM))


def score_kernel(plan, turns, known, first, depth, *refs):
    comes, refs = refs[:len(turns)], refs[len(turns):]
    if first:
        square_ref, other_ref, weight_ref, refs = *refs[:3], refs[3:]
    else:
        factor_ref, before_ref, refs = *refs[:2], refs[2:]
    older, refs = refs[:len(known)], refs[len(known):]
    if first:
        scored_ref, stat_ref, factor_ref, pick = refs
        factor = weight_ref[...] / jnp.sqrt((square_ref[...] + other_ref[...]) / depth + NORM_EPS)
        for i in range(factor.shape[0]):
            column = jnp.sum(jnp.where(diagonal(), factor[i:i + 1, :], 0.0), axis=1, keepdims=True)
            factor_ref[i * 128:(i + 1) * 128, :] = column
    else:
        scored_ref, stat_ref, pick = refs
    blocks = block_readers(known, older)
    stats = []
    for b, turn in enumerate(turns):
        keep = gather_block(plan, plan.take, turn, blocks, pick)
        raw = keep.astype(jnp.float32) + comes[b][...].astype(jnp.float32)
        scored = raw * factor_ref[...]
        scored_ref[b] = scored
        mean = jnp.sum(scored, axis=0, keepdims=True) / scored.shape[0]
        centered = scored - mean
        both = jnp.concatenate([mean, jnp.sum(centered * centered, axis=0, keepdims=True)], axis=0)
        if first:
            stat_ref[b] = both
        else:
            stats.append(both)
    if not first:
        stats = [before_ref[b] for b in range(before_ref.shape[0])] + stats
        lane = lax.broadcasted_iota(jnp.int32, (2, 128), 1)
        codes = [plan.packed(plan.place, half) for half in range(2)]
        for j in range(plan.turns):
            halves = []
            for half in range(2):
                index = entry(codes[half], j)
                value = stats[0]
                for m in range(1, len(stats)):
                    value = jnp.where(index == m, stats[m], value)
                halves.append(value)
            stat_ref[:, j * 128:(j + 1) * 128] = jnp.where(lane < 64, halves[0], halves[1])


def score_call(plan, turns, comes, known, depth, squares=None, factor=None, before=None):
    rows = comes[0].shape[0]
    first = squares is not None
    n = len(turns)
    stat = (n, 2, 128) if first else (2, plan.turns * 128)
    args = list(comes) + (list(squares) if first else [factor, before]) + [a for _, a in known]
    out_shape = [jax.ShapeDtypeStruct((n, rows, 128), jnp.float32), jax.ShapeDtypeStruct(stat, jnp.float32)]
    if first:
        out_shape.append(jax.ShapeDtypeStruct((rows, 1), jnp.float32))
    return pl.pallas_call(
        functools.partial(score_kernel, plan, turns, known, first, depth),
        out_shape=out_shape,
        in_specs=[VMEM] * len(args),
        out_specs=[VMEM] * len(out_shape),
        scratch_shapes=[pltpu.VMEM((2, rows, 128), jnp.bfloat16)],
        compiler_params=pltpu.CompilerParams(vmem_limit_bytes=8 * 1024 * 1024),
        cost_estimate=pl.CostEstimate(flops=8 * n * rows * 128, bytes_accessed=12 * n * rows * 128, transcendentals=0),
    )(*args)


def finish_kernel(plan, count, own_ref, back_ref, early_ref, late_ref, out_ref):
    lane = lax.broadcasted_iota(jnp.int32, late_ref.shape[1:], 1)
    codes = [plan.packed(plan.place, half) for half in range(2)]
    early = early_ref.shape[0]
    stat = jnp.where(lax.axis_index("rows") % 2 == 1, own_ref[...], back_ref[...])
    mean, scale = stat[0:1, :], lax.rsqrt(stat[1:2, :] / count + VAR_EPS)
    for j in range(plan.turns):
        halves = []
        for half in range(2):
            index = entry(codes[half], j)
            value = early_ref[jnp.minimum(index, early - 1)]
            halves.append(jnp.where(index < early, value, late_ref[0]))
        value = jnp.where(lane < 64, halves[0], halves[1])
        columns = slice(j * 128, (j + 1) * 128)
        out_ref[:, columns] = ((value - mean[:, columns]) * scale[:, columns]).astype(jnp.bfloat16)


def finish_call(plan, count, own, back, early, late):
    rows = late.shape[1]
    width = plan.turns * 128
    return pl.pallas_call(
        functools.partial(finish_kernel, plan, count),
        out_shape=jax.ShapeDtypeStruct((rows, width), jnp.bfloat16),
        in_specs=[VMEM] * 4,
        out_specs=VMEM,
        compiler_params=pltpu.CompilerParams(vmem_limit_bytes=8 * 1024 * 1024),
        cost_estimate=pl.CostEstimate(flops=2 * rows * width, bytes_accessed=6 * rows * width, transcendentals=0),
    )(own, back, early, late)


def product_groups(plan):
    groups, p, m = [], 0, 0
    while p < plan.pairs:
        ready = max(max(plan.options(plan.give, half, m)) for half in range(2))
        n = 2 if p == 0 or p + 1 == ready else 1
        done = p + n > ready
        groups.append((p, n, m if done else None))
        m += done
        p += n
    return groups


def ring_body(planes, gradients, queries, loss_weight):
    plan = Plan(planes)
    nodes, far = plan.nodes, plan.far
    rows_here, depth = gradients.shape
    feature_count = depth * 2

    def device(node, c):
        z, x = plan.order[node % nodes]
        return (z * 2 + x) * 2 + c

    swap = [(r, r ^ 1) for r in range(2 * nodes)]
    turn = [(device(n, 0), device(n + 1, 0)) for n in range(nodes)]
    turn += [(device(n, 1), device(n - 1, 1)) for n in range(nodes)]

    def cross(value):
        return lax.ppermute(value, "feat", [(0, 1), (1, 0)])

    ring = [queries, lax.ppermute(queries, "rows", swap)]
    for _ in range(1, 2 * far):
        ring.append(lax.ppermute(ring[-2], "rows", turn))
    arrived = [([queries, ring[1]], [True, False])]
    for k in range(1, 2 * far):
        arrived.append(([ring[k + 1], lax.ppermute(ring[k + 1], "rows", swap)], [k % 2 == 1, k % 2 == 0]))

    gradients, squares = load_call(gradients)
    squares = (squares, cross(squares), loss_weight.reshape(rows_here // 128, 128))

    known, comes = [], []
    for p, n, m in product_groups(plan):
        units, sources = [], []
        for u, s in arrived[p:p + n]:
            units, sources = units + u, sources + s
        out = product_call(plan, gradients, units, sources, known, m)
        known.append((n, out[0]))
        if m is not None:
            comes.append(cross(out[2]))
        gradients = out[1]
    last = len(comes) - 1
    early, stat, factor = score_call(plan, list(range(last)), comes[:last], known, feature_count, squares)
    late, stat = score_call(plan, [last], comes[last:], known, feature_count, None, factor, stat)

    chips = [r for r in range(2 * nodes) if r % 2 == 1]
    ways = [[(r - 1, r) for r in chips]]
    step = 2
    while step < 2 * nodes:
        ways.append([(r, r ^ step) for r in chips])
        step *= 2
    mean, spread = stat[0:1], stat[1:2]
    count = rows_here
    for pairs in ways:
        come = lax.ppermute(jnp.concatenate([mean, spread], axis=0), "rows", pairs)
        gap = come[0:1] - mean
        mean = 0.5 * (mean + come[0:1])
        spread = spread + come[1:2] + (0.5 * count) * (gap * gap)
        count *= 2
    stat = jnp.concatenate([mean, spread], axis=0)
    back = lax.ppermute(stat, "rows", [(r, r - 1) for r in chips])
    return finish_call(plan, count, stat, back, early, late)


def solution(mesh):
    in_specs = (P("rows", "feat"), P("rows", "feat"), P("rows"))
    out_specs = P("rows", "feat")
    rows, feat = mesh.shape["rows"], mesh.shape["feat"]
    planes = rows // 4
    fits = rows == 4 * planes and planes in (2, 4) and feat == 2

    def body(gradients, queries, loss_weight):
        if fits and 2 * queries.shape[0] == 128 and gradients.shape[0] % 256 == 0:
            return ring_body(planes, gradients, queries, loss_weight)
        return plain_body(gradients, queries, loss_weight)

    return jax.shard_map(body, mesh=mesh, in_specs=in_specs, out_specs=out_specs, check_vma=False)
```

```python
import functools

import jax
import jax.numpy as jnp
from jax import lax
from jax.experimental import pallas as pl
from jax.experimental.pallas import tpu as pltpu
from jax.sharding import PartitionSpec as P


NORM_EPS = 1e-06
VAR_EPS = 1e-05
VMEM = pl.BlockSpec(memory_space=pltpu.VMEM)
NT = (((1,), (1,)), ((), ()))


def plain_body(gradients, queries, loss_weight):
    rows_here = gradients.shape[0]
    total_rows = rows_here * lax.axis_size("rows")
    feature_count = gradients.shape[1] * lax.axis_size("feat")
    local_squares = jnp.sum(jnp.square(gradients.astype(jnp.float32)), axis=1)
    squares = lax.psum(local_squares, "feat")
    product = lax.dot_general(
        gradients,
        lax.all_gather(queries, "rows", axis=0, tiled=True),
        NT,
        preferred_element_type=jnp.float32,
    )
    raw = lax.psum_scatter(
        product.astype(jnp.bfloat16), "feat", scatter_dimension=1, tiled=True
    ).astype(jnp.float32)
    factor = loss_weight / jnp.sqrt(squares / feature_count + NORM_EPS)
    scored = raw * factor[:, None]
    column_mean = lax.psum(jnp.sum(scored, axis=0), "rows") / total_rows
    centered = scored - column_mean[None, :]
    square_sums = lax.psum(jnp.sum(centered * centered, axis=0), "rows")
    column_var = square_sums / total_rows
    return (centered * lax.rsqrt(column_var + VAR_EPS)[None, :]).astype(jnp.bfloat16)


def ring_order(planes):
    return [(z, 0) for z in range(planes)] + [(z, 1) for z in range(planes - 1, -1, -1)]


class Plan:
    def __init__(self, planes):
        self.order = ring_order(planes)
        self.nodes = len(self.order)
        self.far = self.nodes // 2
        self.pairs = 2 * self.far
        self.turns = self.pairs // 2
        self.give, self.take, self.place = {}, {}, {}
        for n, (z, x) in enumerate(self.order):
            for f in range(2):
                key = (z * 2 + x) * 2 + f
                for half in range(2):
                    mine, other = [], []
                    spot = [0] * self.turns
                    for p, o in enumerate(self.offsets(n, half)):
                        oz, ox = self.order[(n + o) % self.nodes]
                        chip = oz * 2 + ox
                        if chip // self.turns == f:
                            spot[chip % self.turns] = len(mine)
                            mine.append(p)
                        else:
                            other.append(p)
                    self.give[key, half] = other
                    self.take[key, half] = mine
                    self.place[key, half] = spot

    def offsets(self, n, half):
        out = [0]
        for s in range(1, self.far):
            first = -s if (n + s + half) % 2 == 0 else s
            out += [first, -first]
        return out + [self.far]

    def packed(self, table, half):
        key = (lax.axis_index("rows") // 2) * 2 + lax.axis_index("feat")
        codes = [sum(v << (4 * m) for m, v in enumerate(table[k, half])) for k in range(2 * self.nodes)]
        code = jnp.int32(codes[0])
        for k in range(1, 2 * self.nodes):
            code = jnp.where(key == k, jnp.int32(codes[k]), code)
        return code

    def options(self, table, half, m):
        return sorted({table[k, half][m] for k in range(2 * self.nodes)})


def entry(code, m):
    return (code >> (4 * m)) & 15


def gather_block(plan, table, m, blocks, held):
    for half in range(2):
        index = entry(plan.packed(table, half), m)
        for p in plan.options(table, half, m):
            @pl.when(index == p)
            def _(half=half, p=p):
                held[half] = blocks[p]()
    lane = lax.broadcasted_iota(jnp.int32, held.shape[1:], 1)
    return jnp.where(lane < held.shape[2] // 2, held[0], held[1])


def product_kernel(plan, sources, count, turn, known, grad_ref, *refs):
    units, refs = refs[:count], refs[count:]
    older, refs = refs[:len(known)], refs[len(known):]
    out_ref, refs = refs[0], refs[2:]
    if turn is not None:
        send_ref, held, pick = refs
    else:
        (held,) = refs
    shard = units[0].shape[0]
    core = lax.axis_index("rows") % 2
    for k in range(count):
        pair, same = k // 2, sources[k]
        spot = pair * 2 + (core if same else 1 - core)
        held[pl.ds(pl.multiple_of(spot * shard, shard), shard), :] = units[k][...]
    product = lax.dot_general(grad_ref[...], held[...], NT, preferred_element_type=jnp.float32)
    for b in range(out_ref.shape[0]):
        out_ref[b] = product[:, b * 128:(b + 1) * 128].astype(jnp.bfloat16)
    if turn is not None:
        blocks = block_readers(known, older)
        first = sum(n for n, _ in known) if known else 0
        for b in range(out_ref.shape[0]):
            blocks[first + b] = lambda b=b: out_ref[b]
        send_ref[...] = gather_block(plan, plan.give, turn, blocks, pick)


def block_readers(known, refs):
    blocks, p = {}, 0
    for (n, _), ref in zip(known, refs):
        for b in range(n):
            blocks[p] = lambda ref=ref, b=b: ref[b]
            p += 1
    return blocks


def product_call(plan, gradients, units, sources, known=(), turn=None):
    rows, depth = gradients.shape
    shard = units[0].shape[0]
    count = len(units)
    n = count // 2
    out_shape = [
        jax.ShapeDtypeStruct((n, rows, 128), jnp.bfloat16),
        jax.ShapeDtypeStruct(gradients.shape, gradients.dtype),
    ]
    scratch = [pltpu.VMEM((count * shard, depth), jnp.bfloat16)]
    if turn is None:
        known = ()
    else:
        out_shape.append(jax.ShapeDtypeStruct((rows, 128), jnp.bfloat16))
        scratch.append(pltpu.VMEM((2, rows, 128), jnp.bfloat16))
    known = list(known)
    return pl.pallas_call(
        functools.partial(product_kernel, plan, sources, count, turn, known),
        out_shape=out_shape,
        in_specs=[VMEM] * (1 + count + len(known)),
        out_specs=[VMEM] * len(out_shape),
        scratch_shapes=scratch,
        input_output_aliases={0: 1},
        compiler_params=pltpu.CompilerParams(vmem_limit_bytes=12 * 1024 * 1024),
        cost_estimate=pl.CostEstimate(
            flops=2 * rows * depth * count * shard, bytes_accessed=2 * rows * depth, transcendentals=0
        ),
    )(gradients, *units, *[a for _, a in known])


def diagonal():
    return lax.broadcasted_iota(jnp.int32, (128, 128), 0) == lax.broadcasted_iota(jnp.int32, (128, 128), 1)


def load_kernel(parts, grad_ref, held_ref, square_ref, sums_ref, sem):
    rows, depth = held_ref.shape
    piece = rows // parts
    copies = [
        pltpu.make_async_copy(grad_ref.at[pl.ds(k * piece, piece)], held_ref.at[pl.ds(k * piece, piece)], sem.at[k])
        for k in range(parts)
    ]
    for copy in copies:
        copy.start()
    for k, copy in enumerate(copies):
        copy.wait()

        def step(i, carry, k=k):
            here = pl.ds(pl.multiple_of(k * piece + i * 64, 64), 64)
            total = jnp.zeros((64, 128), jnp.float32)
            for c in range(depth // 128):
                wide = held_ref[here, c * 128:(c + 1) * 128].astype(jnp.float32)
                total = total + wide * wide
            sums_ref[here, :] = jnp.sum(total, axis=1, keepdims=True)
            return carry

        lax.fori_loop(0, piece // 64, step, 0)
    for i in range(square_ref.shape[0]):
        column = sums_ref[i * 128:(i + 1) * 128, :]
        square_ref[i:i + 1, :] = jnp.sum(jnp.where(diagonal(), column, 0.0), axis=0, keepdims=True)


def load_call(gradients, parts=4):
    rows, depth = gradients.shape
    return pl.pallas_call(
        functools.partial(load_kernel, parts),
        out_shape=[
            jax.ShapeDtypeStruct((rows, depth), gradients.dtype),
            jax.ShapeDtypeStruct((rows // 128, 128), jnp.float32),
        ],
        in_specs=[pl.BlockSpec(memory_space=pltpu.HBM)],
        out_specs=[VMEM, VMEM],
        scratch_shapes=[pltpu.VMEM((rows, 1), jnp.float32), pltpu.SemaphoreType.DMA((parts,))],
        compiler_params=pltpu.CompilerParams(vmem_limit_bytes=8 * 1024 * 1024),
        cost_estimate=pl.CostEstimate(flops=2 * rows * depth, bytes_accessed=2 * rows * depth, transcendentals=0),
    )(pltpu.with_memory_space_constraint(gradients, pltpu.HBM))


def score_kernel(plan, turns, known, first, depth, *refs):
    comes, refs = refs[:len(turns)], refs[len(turns):]
    if first:
        square_ref, other_ref, weight_ref, refs = *refs[:3], refs[3:]
    else:
        factor_ref, before_ref, refs = *refs[:2], refs[2:]
    older, refs = refs[:len(known)], refs[len(known):]
    if first:
        scored_ref, stat_ref, factor_ref, pick = refs
        factor = weight_ref[...] / jnp.sqrt((square_ref[...] + other_ref[...]) / depth + NORM_EPS)
        for i in range(factor.shape[0]):
            column = jnp.sum(jnp.where(diagonal(), factor[i:i + 1, :], 0.0), axis=1, keepdims=True)
            factor_ref[i * 128:(i + 1) * 128, :] = column
    else:
        scored_ref, stat_ref, pick = refs
    blocks = block_readers(known, older)
    stats = []
    for b, turn in enumerate(turns):
        keep = gather_block(plan, plan.take, turn, blocks, pick)
        raw = keep.astype(jnp.float32) + comes[b][...].astype(jnp.float32)
        scored = raw * factor_ref[...]
        scored_ref[b] = scored
        mean = jnp.sum(scored, axis=0, keepdims=True) / scored.shape[0]
        centered = scored - mean
        both = jnp.concatenate([mean, jnp.sum(centered * centered, axis=0, keepdims=True)], axis=0)
        if first:
            stat_ref[b] = both
        else:
            stats.append(both)
    if not first:
        stats = [before_ref[b] for b in range(before_ref.shape[0])] + stats
        lane = lax.broadcasted_iota(jnp.int32, (2, 128), 1)
        codes = [plan.packed(plan.place, half) for half in range(2)]
        for j in range(plan.turns):
            halves = []
            for half in range(2):
                index = entry(codes[half], j)
                value = stats[0]
                for m in range(1, len(stats)):
                    value = jnp.where(index == m, stats[m], value)
                halves.append(value)
            stat_ref[:, j * 128:(j + 1) * 128] = jnp.where(lane < 64, halves[0], halves[1])


def score_call(plan, turns, comes, known, depth, squares=None, factor=None, before=None):
    rows = comes[0].shape[0]
    first = squares is not None
    n = len(turns)
    stat = (n, 2, 128) if first else (2, plan.turns * 128)
    args = list(comes) + (list(squares) if first else [factor, before]) + [a for _, a in known]
    out_shape = [jax.ShapeDtypeStruct((n, rows, 128), jnp.float32), jax.ShapeDtypeStruct(stat, jnp.float32)]
    if first:
        out_shape.append(jax.ShapeDtypeStruct((rows, 1), jnp.float32))
    return pl.pallas_call(
        functools.partial(score_kernel, plan, turns, known, first, depth),
        out_shape=out_shape,
        in_specs=[VMEM] * len(args),
        out_specs=[VMEM] * len(out_shape),
        scratch_shapes=[pltpu.VMEM((2, rows, 128), jnp.bfloat16)],
        compiler_params=pltpu.CompilerParams(vmem_limit_bytes=8 * 1024 * 1024),
        cost_estimate=pl.CostEstimate(flops=8 * n * rows * 128, bytes_accessed=12 * n * rows * 128, transcendentals=0),
    )(*args)


def arrange_kernel(plan, early_ref, late_ref, out_ref):
    lane = lax.broadcasted_iota(jnp.int32, late_ref.shape[1:], 1)
    codes = [plan.packed(plan.place, half) for half in range(2)]
    early = early_ref.shape[0]
    for j in range(plan.turns):
        halves = []
        for half in range(2):
            index = entry(codes[half], j)
            value = early_ref[jnp.minimum(index, early - 1)]
            halves.append(jnp.where(index < early, value, late_ref[0]))
        out_ref[:, j * 128:(j + 1) * 128] = jnp.where(lane < 64, halves[0], halves[1])


def arrange_call(plan, early, late):
    rows, width = late.shape[1], plan.turns * 128
    return pl.pallas_call(
        functools.partial(arrange_kernel, plan),
        out_shape=jax.ShapeDtypeStruct((rows, width), jnp.float32),
        in_specs=[VMEM] * 2,
        out_specs=VMEM,
        compiler_params=pltpu.CompilerParams(vmem_limit_bytes=8 * 1024 * 1024),
        cost_estimate=pl.CostEstimate(flops=rows * width, bytes_accessed=8 * rows * width, transcendentals=0),
    )(early, late)


def finish_kernel(count, stat_ref, scored_ref, out_ref):
    rows = out_ref.shape[0]
    here = pl.ds(pl.multiple_of(pl.program_id(0) * rows, rows), rows)
    scale = lax.rsqrt(stat_ref[1:2, :] / count + VAR_EPS)
    out_ref[...] = ((scored_ref[here, :] - stat_ref[0:1, :]) * scale).astype(jnp.bfloat16)


def finish_call(count, stat, scored, steps=4):
    rows, width = scored.shape
    return pl.pallas_call(
        functools.partial(finish_kernel, count),
        grid=(steps,),
        out_shape=jax.ShapeDtypeStruct((rows, width), jnp.bfloat16),
        in_specs=[VMEM] * 2,
        out_specs=pl.BlockSpec((rows // steps, width), lambda i: (i, 0)),
        compiler_params=pltpu.CompilerParams(vmem_limit_bytes=8 * 1024 * 1024),
        cost_estimate=pl.CostEstimate(flops=2 * rows * width, bytes_accessed=6 * rows * width, transcendentals=0),
    )(stat, scored)


def product_groups(plan):
    groups, p, m = [], 0, 0
    while p < plan.pairs:
        ready = max(max(plan.options(plan.give, half, m)) for half in range(2))
        n = 2 if p == 0 or p + 1 == ready else 1
        done = p + n > ready
        groups.append((p, n, m if done else None))
        m += done
        p += n
    return groups


def ring_body(planes, gradients, queries, loss_weight):
    plan = Plan(planes)
    nodes, far = plan.nodes, plan.far
    rows_here, depth = gradients.shape
    feature_count = depth * 2

    def device(node, c):
        z, x = plan.order[node % nodes]
        return (z * 2 + x) * 2 + c

    swap = [(r, r ^ 1) for r in range(2 * nodes)]
    turn = [(device(n, n % 2), device(n + 1, (n + 1) % 2)) for n in range(nodes)]
    turn += [(device(n, 1 - n % 2), device(n - 1, n % 2)) for n in range(nodes)]

    def cross(value):
        return lax.ppermute(value, "feat", [(0, 1), (1, 0)])

    ring = [queries, lax.ppermute(queries, "rows", swap)]
    for _ in range(1, 2 * far):
        ring.append(lax.ppermute(ring[-2], "rows", turn))
    arrived = [([queries, ring[1]], [True, False])]
    for k in range(1, 2 * far):
        same = [(k + 1) // 2 % 2 == 0, (k + 1) // 2 % 2 == 1]
        arrived.append(([ring[k + 1], lax.ppermute(ring[k + 1], "rows", swap)], same if k % 2 else same[::-1]))

    gradients, squares = load_call(gradients)
    squares = (squares, cross(squares), loss_weight.reshape(rows_here // 128, 128))

    known, comes = [], []
    for p, n, m in product_groups(plan):
        units, sources = [], []
        for u, s in arrived[p:p + n]:
            units, sources = units + u, sources + s
        out = product_call(plan, gradients, units, sources, known, m)
        known.append((n, out[0]))
        if m is not None:
            comes.append(cross(out[2]))
        gradients = out[1]
    last = len(comes) - 1
    early, stat, factor = score_call(plan, list(range(last)), comes[:last], known, feature_count, squares)
    late, stat = score_call(plan, [last], comes[last:], known, feature_count, None, factor, stat)

    scored = arrange_call(plan, early, late)
    mean, spread = stat[0:1], stat[1:2]
    count, step = rows_here, 1
    while step < 2 * nodes:
        pairs = [(r, r ^ (step | 1)) for r in range(2 * nodes)]
        come = lax.ppermute(jnp.concatenate([mean, spread], axis=0), "rows", pairs)
        gap = come[0:1] - mean
        mean = 0.5 * (mean + come[0:1])
        spread = spread + come[1:2] + (0.5 * count) * (gap * gap)
        count *= 2
        step *= 2
    return finish_call(count, jnp.concatenate([mean, spread], axis=0), scored)


def solution(mesh):
    in_specs = (P("rows", "feat"), P("rows", "feat"), P("rows"))
    out_specs = P("rows", "feat")
    rows, feat = mesh.shape["rows"], mesh.shape["feat"]
    planes = rows // 4
    fits = rows == 4 * planes and planes in (2, 4) and feat == 2

    def body(gradients, queries, loss_weight):
        if fits and 2 * queries.shape[0] == 128 and gradients.shape[0] % 256 == 0:
            return ring_body(planes, gradients, queries, loss_weight)
        return plain_body(gradients, queries, loss_weight)

    return jax.shard_map(body, mesh=mesh, in_specs=in_specs, out_specs=out_specs, check_vma=False)
```

```python
import functools

import jax
import jax.numpy as jnp
from jax import lax
from jax.experimental import pallas as pl
from jax.experimental.pallas import tpu as pltpu
from jax.sharding import PartitionSpec as P


NORM_EPS = 1e-06
VAR_EPS = 1e-05
VMEM = pl.BlockSpec(memory_space=pltpu.VMEM)
NT = (((1,), (1,)), ((), ()))


def plain_body(gradients, queries, loss_weight):
    rows_here = gradients.shape[0]
    total_rows = rows_here * lax.axis_size("rows")
    feature_count = gradients.shape[1] * lax.axis_size("feat")
    local_squares = jnp.sum(jnp.square(gradients.astype(jnp.float32)), axis=1)
    squares = lax.psum(local_squares, "feat")
    product = lax.dot_general(
        gradients,
        lax.all_gather(queries, "rows", axis=0, tiled=True),
        NT,
        preferred_element_type=jnp.float32,
    )
    raw = lax.psum_scatter(
        product.astype(jnp.bfloat16), "feat", scatter_dimension=1, tiled=True
    ).astype(jnp.float32)
    factor = loss_weight / jnp.sqrt(squares / feature_count + NORM_EPS)
    scored = raw * factor[:, None]
    column_mean = lax.psum(jnp.sum(scored, axis=0), "rows") / total_rows
    centered = scored - column_mean[None, :]
    square_sums = lax.psum(jnp.sum(centered * centered, axis=0), "rows")
    column_var = square_sums / total_rows
    return (centered * lax.rsqrt(column_var + VAR_EPS)[None, :]).astype(jnp.bfloat16)


def ring_order(planes):
    return [(z, 0) for z in range(planes)] + [(z, 1) for z in range(planes - 1, -1, -1)]


class Plan:
    def __init__(self, planes):
        self.order = ring_order(planes)
        self.nodes = len(self.order)
        self.far = self.nodes // 2
        self.pairs = 2 * self.far
        self.turns = self.pairs // 2
        self.give, self.take, self.place = {}, {}, {}
        for n, (z, x) in enumerate(self.order):
            for f in range(2):
                key = (z * 2 + x) * 2 + f
                for half in range(2):
                    mine, other = [], []
                    spot = [0] * self.turns
                    for p, o in enumerate(self.offsets(n, half)):
                        oz, ox = self.order[(n + o) % self.nodes]
                        chip = oz * 2 + ox
                        if chip // self.turns == f:
                            spot[chip % self.turns] = len(mine)
                            mine.append(p)
                        else:
                            other.append(p)
                    self.give[key, half] = other
                    self.take[key, half] = mine
                    self.place[key, half] = spot

    def offsets(self, n, half):
        out = [0]
        for s in range(1, self.far):
            first = -s if (n + s + half) % 2 == 0 else s
            out += [first, -first]
        return out + [self.far]

    def packed(self, table, half):
        key = (lax.axis_index("rows") // 2) * 2 + lax.axis_index("feat")
        codes = [sum(v << (4 * m) for m, v in enumerate(table[k, half])) for k in range(2 * self.nodes)]
        code = jnp.int32(codes[0])
        for k in range(1, 2 * self.nodes):
            code = jnp.where(key == k, jnp.int32(codes[k]), code)
        return code

    def options(self, table, half, m):
        return sorted({table[k, half][m] for k in range(2 * self.nodes)})


def entry(code, m):
    return (code >> (4 * m)) & 15


def gather_block(plan, table, m, blocks, held):
    for half in range(2):
        index = entry(plan.packed(table, half), m)
        for p in plan.options(table, half, m):
            @pl.when(index == p)
            def _(half=half, p=p):
                held[half] = blocks[p]()
    lane = lax.broadcasted_iota(jnp.int32, held.shape[1:], 1)
    return jnp.where(lane < held.shape[2] // 2, held[0], held[1])


def product_kernel(plan, sources, count, turn, known, grad_ref, *refs):
    units, refs = refs[:count], refs[count:]
    older, refs = refs[:len(known)], refs[len(known):]
    out_ref, refs = refs[0], refs[2:]
    if turn is not None:
        send_ref, held, pick = refs
    else:
        (held,) = refs
    shard = units[0].shape[0]
    core = lax.axis_index("rows") % 2
    for k in range(count):
        pair, same = k // 2, sources[k]
        spot = pair * 2 + (core if same else 1 - core)
        held[pl.ds(pl.multiple_of(spot * shard, shard), shard), :] = units[k][...]
    product = lax.dot_general(grad_ref[...], held[...], NT, preferred_element_type=jnp.float32)
    for b in range(out_ref.shape[0]):
        out_ref[b] = product[:, b * 128:(b + 1) * 128].astype(jnp.bfloat16)
    if turn is not None:
        blocks = block_readers(known, older)
        first = sum(n for n, _ in known) if known else 0
        for b in range(out_ref.shape[0]):
            blocks[first + b] = lambda b=b: out_ref[b]
        send_ref[...] = gather_block(plan, plan.give, turn, blocks, pick)


def block_readers(known, refs):
    blocks, p = {}, 0
    for (n, _), ref in zip(known, refs):
        for b in range(n):
            blocks[p] = lambda ref=ref, b=b: ref[b]
            p += 1
    return blocks


def product_call(plan, gradients, units, sources, known=(), turn=None):
    rows, depth = gradients.shape
    shard = units[0].shape[0]
    count = len(units)
    n = count // 2
    out_shape = [
        jax.ShapeDtypeStruct((n, rows, 128), jnp.bfloat16),
        jax.ShapeDtypeStruct(gradients.shape, gradients.dtype),
    ]
    scratch = [pltpu.VMEM((count * shard, depth), jnp.bfloat16)]
    if turn is None:
        known = ()
    else:
        out_shape.append(jax.ShapeDtypeStruct((rows, 128), jnp.bfloat16))
        scratch.append(pltpu.VMEM((2, rows, 128), jnp.bfloat16))
    known = list(known)
    return pl.pallas_call(
        functools.partial(product_kernel, plan, sources, count, turn, known),
        out_shape=out_shape,
        in_specs=[VMEM] * (1 + count + len(known)),
        out_specs=[VMEM] * len(out_shape),
        scratch_shapes=scratch,
        input_output_aliases={0: 1},
        compiler_params=pltpu.CompilerParams(vmem_limit_bytes=12 * 1024 * 1024),
        cost_estimate=pl.CostEstimate(
            flops=2 * rows * depth * count * shard, bytes_accessed=2 * rows * depth, transcendentals=0
        ),
    )(gradients, *units, *[a for _, a in known])


def diagonal():
    return lax.broadcasted_iota(jnp.int32, (128, 128), 0) == lax.broadcasted_iota(jnp.int32, (128, 128), 1)


def load_kernel(parts, grad_ref, held_ref, square_ref, sums_ref, sem):
    rows, depth = held_ref.shape
    piece = rows // parts
    copies = [
        pltpu.make_async_copy(grad_ref.at[pl.ds(k * piece, piece)], held_ref.at[pl.ds(k * piece, piece)], sem.at[k])
        for k in range(parts)
    ]
    for copy in copies:
        copy.start()
    for k, copy in enumerate(copies):
        copy.wait()

        def step(i, carry, k=k):
            here = pl.ds(pl.multiple_of(k * piece + i * 64, 64), 64)
            total = jnp.zeros((64, 128), jnp.float32)
            for c in range(depth // 128):
                wide = held_ref[here, c * 128:(c + 1) * 128].astype(jnp.float32)
                total = total + wide * wide
            sums_ref[here, :] = jnp.sum(total, axis=1, keepdims=True)
            return carry

        lax.fori_loop(0, piece // 64, step, 0)
    for i in range(square_ref.shape[0]):
        column = sums_ref[i * 128:(i + 1) * 128, :]
        square_ref[i:i + 1, :] = jnp.sum(jnp.where(diagonal(), column, 0.0), axis=0, keepdims=True)


def load_call(gradients, parts=8):
    rows, depth = gradients.shape
    return pl.pallas_call(
        functools.partial(load_kernel, parts),
        out_shape=[
            jax.ShapeDtypeStruct((rows, depth), gradients.dtype),
            jax.ShapeDtypeStruct((rows // 128, 128), jnp.float32),
        ],
        in_specs=[pl.BlockSpec(memory_space=pltpu.HBM)],
        out_specs=[VMEM, VMEM],
        scratch_shapes=[pltpu.VMEM((rows, 1), jnp.float32), pltpu.SemaphoreType.DMA((parts,))],
        compiler_params=pltpu.CompilerParams(vmem_limit_bytes=8 * 1024 * 1024),
        cost_estimate=pl.CostEstimate(flops=2 * rows * depth, bytes_accessed=2 * rows * depth, transcendentals=0),
    )(pltpu.with_memory_space_constraint(gradients, pltpu.HBM))


def score_kernel(plan, turns, known, first, depth, *refs):
    comes, refs = refs[:len(turns)], refs[len(turns):]
    if first:
        square_ref, other_ref, weight_ref, refs = *refs[:3], refs[3:]
    else:
        factor_ref, before_ref, refs = *refs[:2], refs[2:]
    older, refs = refs[:len(known)], refs[len(known):]
    if first:
        scored_ref, stat_ref, factor_ref, pick = refs
        factor = weight_ref[...] / jnp.sqrt((square_ref[...] + other_ref[...]) / depth + NORM_EPS)
        for i in range(factor.shape[0]):
            column = jnp.sum(jnp.where(diagonal(), factor[i:i + 1, :], 0.0), axis=1, keepdims=True)
            factor_ref[i * 128:(i + 1) * 128, :] = column
    else:
        scored_ref, stat_ref, pick = refs
    blocks = block_readers(known, older)
    stats = []
    for b, turn in enumerate(turns):
        keep = gather_block(plan, plan.take, turn, blocks, pick)
        raw = keep.astype(jnp.float32) + comes[b][...].astype(jnp.float32)
        scored = raw * factor_ref[...]
        scored_ref[b] = scored
        mean = jnp.sum(scored, axis=0, keepdims=True) / scored.shape[0]
        centered = scored - mean
        both = jnp.concatenate([mean, jnp.sum(centered * centered, axis=0, keepdims=True)], axis=0)
        if first:
            stat_ref[b] = both
        else:
            stats.append(both)
    if not first:
        stats = [before_ref[b] for b in range(before_ref.shape[0])] + stats
        lane = lax.broadcasted_iota(jnp.int32, (2, 128), 1)
        codes = [plan.packed(plan.place, half) for half in range(2)]
        for j in range(plan.turns):
            halves = []
            for half in range(2):
                index = entry(codes[half], j)
                value = stats[0]
                for m in range(1, len(stats)):
                    value = jnp.where(index == m, stats[m], value)
                halves.append(value)
            stat_ref[:, j * 128:(j + 1) * 128] = jnp.where(lane < 64, halves[0], halves[1])


def score_call(plan, turns, comes, known, depth, squares=None, factor=None, before=None):
    rows = comes[0].shape[0]
    first = squares is not None
    n = len(turns)
    stat = (n, 2, 128) if first else (2, plan.turns * 128)
    args = list(comes) + (list(squares) if first else [factor, before]) + [a for _, a in known]
    out_shape = [jax.ShapeDtypeStruct((n, rows, 128), jnp.float32), jax.ShapeDtypeStruct(stat, jnp.float32)]
    if first:
        out_shape.append(jax.ShapeDtypeStruct((rows, 1), jnp.float32))
    return pl.pallas_call(
        functools.partial(score_kernel, plan, turns, known, first, depth),
        out_shape=out_shape,
        in_specs=[VMEM] * len(args),
        out_specs=[VMEM] * len(out_shape),
        scratch_shapes=[pltpu.VMEM((2, rows, 128), jnp.bfloat16)],
        compiler_params=pltpu.CompilerParams(vmem_limit_bytes=8 * 1024 * 1024),
        cost_estimate=pl.CostEstimate(flops=8 * n * rows * 128, bytes_accessed=12 * n * rows * 128, transcendentals=0),
    )(*args)


def arrange_kernel(plan, early_ref, late_ref, out_ref):
    lane = lax.broadcasted_iota(jnp.int32, late_ref.shape[1:], 1)
    codes = [plan.packed(plan.place, half) for half in range(2)]
    early = early_ref.shape[0]
    for j in range(plan.turns):
        halves = []
        for half in range(2):
            index = entry(codes[half], j)
            value = early_ref[jnp.minimum(index, early - 1)]
            halves.append(jnp.where(index < early, value, late_ref[0]))
        out_ref[:, j * 128:(j + 1) * 128] = jnp.where(lane < 64, halves[0], halves[1])


def arrange_call(plan, early, late):
    rows, width = late.shape[1], plan.turns * 128
    return pl.pallas_call(
        functools.partial(arrange_kernel, plan),
        out_shape=jax.ShapeDtypeStruct((rows, width), jnp.float32),
        in_specs=[VMEM] * 2,
        out_specs=VMEM,
        compiler_params=pltpu.CompilerParams(vmem_limit_bytes=8 * 1024 * 1024),
        cost_estimate=pl.CostEstimate(flops=rows * width, bytes_accessed=8 * rows * width, transcendentals=0),
    )(early, late)


def finish_kernel(count, stat_ref, scored_ref, out_ref, held, sem):
    scale = lax.rsqrt(stat_ref[1:2, :] / count + VAR_EPS)
    steps, rows = held.shape[0], held.shape[1]
    copies = []
    for i in range(steps):
        here = slice(i * rows, (i + 1) * rows)
        held[i] = ((scored_ref[here, :] - stat_ref[0:1, :]) * scale).astype(jnp.bfloat16)
        copies.append(pltpu.make_async_copy(held.at[i], out_ref.at[pl.ds(i * rows, rows)], sem.at[i]))
        copies[i].start()
    for copy in copies:
        copy.wait()


def finish_call(count, stat, scored, steps=8):
    rows, width = scored.shape
    return pl.pallas_call(
        functools.partial(finish_kernel, count),
        out_shape=jax.ShapeDtypeStruct((rows, width), jnp.bfloat16),
        in_specs=[VMEM] * 2,
        out_specs=pl.BlockSpec(memory_space=pltpu.HBM),
        scratch_shapes=[
            pltpu.VMEM((steps, rows // steps, width), jnp.bfloat16),
            pltpu.SemaphoreType.DMA((steps,)),
        ],
        compiler_params=pltpu.CompilerParams(vmem_limit_bytes=8 * 1024 * 1024),
        cost_estimate=pl.CostEstimate(flops=2 * rows * width, bytes_accessed=6 * rows * width, transcendentals=0),
    )(stat, scored)


def product_groups(plan):
    groups, p, m = [], 0, 0
    while p < plan.pairs:
        ready = max(max(plan.options(plan.give, half, m)) for half in range(2))
        n = 2 if p == 0 or p + 1 == ready else 1
        done = p + n > ready
        groups.append((p, n, m if done else None))
        m += done
        p += n
    return groups


def ring_body(planes, gradients, queries, loss_weight):
    plan = Plan(planes)
    nodes, far = plan.nodes, plan.far
    rows_here, depth = gradients.shape
    feature_count = depth * 2

    def device(node, c):
        z, x = plan.order[node % nodes]
        return (z * 2 + x) * 2 + c

    swap = [(r, r ^ 1) for r in range(2 * nodes)]
    turn = [(device(n, n % 2), device(n + 1, (n + 1) % 2)) for n in range(nodes)]
    turn += [(device(n, 1 - n % 2), device(n - 1, n % 2)) for n in range(nodes)]

    def cross(value):
        return lax.ppermute(value, "feat", [(0, 1), (1, 0)])

    ring = [queries, lax.ppermute(queries, "rows", swap)]
    for _ in range(1, 2 * far):
        ring.append(lax.ppermute(ring[-2], "rows", turn))
    arrived = [([queries, ring[1]], [True, False])]
    for k in range(1, 2 * far):
        same = [(k + 1) // 2 % 2 == 0, (k + 1) // 2 % 2 == 1]
        arrived.append(([ring[k + 1], lax.ppermute(ring[k + 1], "rows", swap)], same if k % 2 else same[::-1]))

    gradients, squares = load_call(gradients)
    squares = (squares, cross(squares), loss_weight.reshape(rows_here // 128, 128))

    known, comes = [], []
    for p, n, m in product_groups(plan):
        units, sources = [], []
        for u, s in arrived[p:p + n]:
            units, sources = units + u, sources + s
        out = product_call(plan, gradients, units, sources, known, m)
        known.append((n, out[0]))
        if m is not None:
            comes.append(cross(out[2]))
        gradients = out[1]
    last = len(comes) - 1
    early, stat, factor = score_call(plan, list(range(last)), comes[:last], known, feature_count, squares)
    late, stat = score_call(plan, [last], comes[last:], known, feature_count, None, factor, stat)

    scored = arrange_call(plan, early, late)
    mean, spread = stat[0:1], stat[1:2]
    count, step = rows_here, 1
    while step < 2 * nodes:
        pairs = [(r, r ^ (step | 1)) for r in range(2 * nodes)]
        come = lax.ppermute(jnp.concatenate([mean, spread], axis=0), "rows", pairs)
        gap = come[0:1] - mean
        mean = 0.5 * (mean + come[0:1])
        spread = spread + come[1:2] + (0.5 * count) * (gap * gap)
        count *= 2
        step *= 2
    return finish_call(count, jnp.concatenate([mean, spread], axis=0), scored)


def solution(mesh):
    in_specs = (P("rows", "feat"), P("rows", "feat"), P("rows"))
    out_specs = P("rows", "feat")
    rows, feat = mesh.shape["rows"], mesh.shape["feat"]
    planes = rows // 4
    fits = rows == 4 * planes and planes in (2, 4) and feat == 2

    def body(gradients, queries, loss_weight):
        if fits and 2 * queries.shape[0] == 128 and gradients.shape[0] % 256 == 0:
            return ring_body(planes, gradients, queries, loss_weight)
        return plain_body(gradients, queries, loss_weight)

    return jax.shard_map(body, mesh=mesh, in_specs=in_specs, out_specs=out_specs, check_vma=False)
```

```python
import functools

import jax
import jax.numpy as jnp
from jax import lax
from jax.experimental import pallas as pl
from jax.experimental.pallas import tpu as pltpu
from jax.sharding import PartitionSpec as P


NORM_EPS = 1e-06
VAR_EPS = 1e-05
VMEM = pl.BlockSpec(memory_space=pltpu.VMEM)
NT = (((1,), (1,)), ((), ()))


def plain_body(gradients, queries, loss_weight):
    rows_here = gradients.shape[0]
    total_rows = rows_here * lax.axis_size("rows")
    feature_count = gradients.shape[1] * lax.axis_size("feat")
    local_squares = jnp.sum(jnp.square(gradients.astype(jnp.float32)), axis=1)
    squares = lax.psum(local_squares, "feat")
    product = lax.dot_general(
        gradients,
        lax.all_gather(queries, "rows", axis=0, tiled=True),
        NT,
        preferred_element_type=jnp.float32,
    )
    raw = lax.psum_scatter(
        product.astype(jnp.bfloat16), "feat", scatter_dimension=1, tiled=True
    ).astype(jnp.float32)
    factor = loss_weight / jnp.sqrt(squares / feature_count + NORM_EPS)
    scored = raw * factor[:, None]
    column_mean = lax.psum(jnp.sum(scored, axis=0), "rows") / total_rows
    centered = scored - column_mean[None, :]
    square_sums = lax.psum(jnp.sum(centered * centered, axis=0), "rows")
    column_var = square_sums / total_rows
    return (centered * lax.rsqrt(column_var + VAR_EPS)[None, :]).astype(jnp.bfloat16)


def ring_order(planes):
    return [(z, 0) for z in range(planes)] + [(z, 1) for z in range(planes - 1, -1, -1)]


class Plan:
    def __init__(self, planes):
        self.order = ring_order(planes)
        self.nodes = len(self.order)
        self.far = self.nodes // 2
        self.pairs = 2 * self.far
        self.turns = self.pairs // 2
        self.give, self.take, self.place = {}, {}, {}
        for n, (z, x) in enumerate(self.order):
            for f in range(2):
                key = (z * 2 + x) * 2 + f
                for half in range(2):
                    mine, other = [], []
                    spot = [0] * self.turns
                    for p, o in enumerate(self.offsets(n, half)):
                        oz, ox = self.order[(n + o) % self.nodes]
                        chip = oz * 2 + ox
                        if chip // self.turns == f:
                            spot[chip % self.turns] = len(mine)
                            mine.append(p)
                        else:
                            other.append(p)
                    self.give[key, half] = other
                    self.take[key, half] = mine
                    self.place[key, half] = spot

    def offsets(self, n, half):
        out = [0]
        for s in range(1, self.far):
            first = -s if (n + s + half) % 2 == 0 else s
            out += [first, -first]
        return out + [self.far]

    def packed(self, table, half):
        key = (lax.axis_index("rows") // 2) * 2 + lax.axis_index("feat")
        codes = [sum(v << (4 * m) for m, v in enumerate(table[k, half])) for k in range(2 * self.nodes)]
        code = jnp.int32(codes[0])
        for k in range(1, 2 * self.nodes):
            code = jnp.where(key == k, jnp.int32(codes[k]), code)
        return code

    def options(self, table, half, m):
        return sorted({table[k, half][m] for k in range(2 * self.nodes)})


def entry(code, m):
    return (code >> (4 * m)) & 15


def gather_block(plan, table, m, blocks, held):
    for half in range(2):
        index = entry(plan.packed(table, half), m)
        for p in plan.options(table, half, m):
            @pl.when(index == p)
            def _(half=half, p=p):
                held[half] = blocks[p]()
    lane = lax.broadcasted_iota(jnp.int32, held.shape[1:], 1)
    return jnp.where(lane < held.shape[2] // 2, held[0], held[1])


def product_kernel(plan, sources, count, turn, known, grad_ref, *refs):
    units, refs = refs[:count], refs[count:]
    older, refs = refs[:len(known)], refs[len(known):]
    out_ref, refs = refs[0], refs[2:]
    if turn is not None:
        send_ref, held, pick = refs
    else:
        (held,) = refs
    shard = units[0].shape[0]
    core = lax.axis_index("rows") % 2
    for k in range(count):
        pair, same = k // 2, sources[k]
        spot = pair * 2 + (core if same else 1 - core)
        held[pl.ds(pl.multiple_of(spot * shard, shard), shard), :] = units[k][...]
    product = lax.dot_general(grad_ref[...], held[...], NT, preferred_element_type=jnp.float32)
    for b in range(out_ref.shape[0]):
        out_ref[b] = product[:, b * 128:(b + 1) * 128].astype(jnp.bfloat16)
    if turn is not None:
        blocks = block_readers(known, older)
        first = sum(n for n, _ in known) if known else 0
        for b in range(out_ref.shape[0]):
            blocks[first + b] = lambda b=b: out_ref[b]
        send_ref[...] = gather_block(plan, plan.give, turn, blocks, pick)


def block_readers(known, refs):
    blocks, p = {}, 0
    for (n, _), ref in zip(known, refs):
        for b in range(n):
            blocks[p] = lambda ref=ref, b=b: ref[b]
            p += 1
    return blocks


def product_call(plan, gradients, units, sources, known=(), turn=None):
    rows, depth = gradients.shape
    shard = units[0].shape[0]
    count = len(units)
    n = count // 2
    out_shape = [
        jax.ShapeDtypeStruct((n, rows, 128), jnp.bfloat16),
        jax.ShapeDtypeStruct(gradients.shape, gradients.dtype),
    ]
    scratch = [pltpu.VMEM((count * shard, depth), jnp.bfloat16)]
    if turn is None:
        known = ()
    else:
        out_shape.append(jax.ShapeDtypeStruct((rows, 128), jnp.bfloat16))
        scratch.append(pltpu.VMEM((2, rows, 128), jnp.bfloat16))
    known = list(known)
    return pl.pallas_call(
        functools.partial(product_kernel, plan, sources, count, turn, known),
        out_shape=out_shape,
        in_specs=[VMEM] * (1 + count + len(known)),
        out_specs=[VMEM] * len(out_shape),
        scratch_shapes=scratch,
        input_output_aliases={0: 1},
        compiler_params=pltpu.CompilerParams(vmem_limit_bytes=12 * 1024 * 1024),
        cost_estimate=pl.CostEstimate(
            flops=2 * rows * depth * count * shard, bytes_accessed=2 * rows * depth, transcendentals=0
        ),
    )(gradients, *units, *[a for _, a in known])


def diagonal():
    return lax.broadcasted_iota(jnp.int32, (128, 128), 0) == lax.broadcasted_iota(jnp.int32, (128, 128), 1)


def load_kernel(parts, grad_ref, held_ref, square_ref, sums_ref, sem):
    rows, depth = held_ref.shape
    piece = rows // parts
    copies = [
        pltpu.make_async_copy(grad_ref.at[pl.ds(k * piece, piece)], held_ref.at[pl.ds(k * piece, piece)], sem.at[k])
        for k in range(parts)
    ]
    for copy in copies:
        copy.start()
    for k, copy in enumerate(copies):
        copy.wait()

        def step(i, carry, k=k):
            here = pl.ds(pl.multiple_of(k * piece + i * 64, 64), 64)
            total = jnp.zeros((64, 128), jnp.float32)
            for c in range(depth // 128):
                wide = held_ref[here, c * 128:(c + 1) * 128].astype(jnp.float32)
                total = total + wide * wide
            sums_ref[here, :] = jnp.sum(total, axis=1, keepdims=True)
            return carry

        lax.fori_loop(0, piece // 64, step, 0)
    for i in range(square_ref.shape[0]):
        column = sums_ref[i * 128:(i + 1) * 128, :]
        square_ref[i:i + 1, :] = jnp.sum(jnp.where(diagonal(), column, 0.0), axis=0, keepdims=True)


def load_call(gradients, parts=8):
    rows, depth = gradients.shape
    return pl.pallas_call(
        functools.partial(load_kernel, parts),
        out_shape=[
            jax.ShapeDtypeStruct((rows, depth), gradients.dtype),
            jax.ShapeDtypeStruct((rows // 128, 128), jnp.float32),
        ],
        in_specs=[pl.BlockSpec(memory_space=pltpu.HBM)],
        out_specs=[VMEM, VMEM],
        scratch_shapes=[pltpu.VMEM((rows, 1), jnp.float32), pltpu.SemaphoreType.DMA((parts,))],
        compiler_params=pltpu.CompilerParams(vmem_limit_bytes=8 * 1024 * 1024),
        cost_estimate=pl.CostEstimate(flops=2 * rows * depth, bytes_accessed=2 * rows * depth, transcendentals=0),
    )(pltpu.with_memory_space_constraint(gradients, pltpu.HBM))


def score_kernel(plan, turns, known, first, depth, *refs):
    comes, refs = refs[:len(turns)], refs[len(turns):]
    if first:
        square_ref, other_ref, weight_ref, refs = *refs[:3], refs[3:]
    else:
        factor_ref, before_ref, kept_ref, refs = *refs[:3], refs[3:]
    older, refs = refs[:len(known)], refs[len(known):]
    if first:
        scored_ref, stat_ref, factor_ref, kept_ref, pick = refs
        factor = weight_ref[...] / jnp.sqrt((square_ref[...] + other_ref[...]) / depth + NORM_EPS)
        for i in range(factor.shape[0]):
            column = jnp.sum(jnp.where(diagonal(), factor[i:i + 1, :], 0.0), axis=1, keepdims=True)
            factor_ref[i * 128:(i + 1) * 128, :] = column
    else:
        scored_ref, stat_ref = refs
    blocks = block_readers(known, older)
    stats = []
    for b, turn in enumerate(turns):
        keep = gather_block(plan, plan.take, turn, blocks, pick).astype(jnp.float32) if first else kept_ref[...]
        raw = keep + comes[b][...].astype(jnp.float32)
        scored = raw * factor_ref[...]
        scored_ref[b] = scored
        mean = jnp.sum(scored, axis=0, keepdims=True) / scored.shape[0]
        centered = scored - mean
        both = jnp.concatenate([mean, jnp.sum(centered * centered, axis=0, keepdims=True)], axis=0)
        if first:
            stat_ref[b] = both
        else:
            stats.append(both)
    if first:
        kept_ref[...] = gather_block(plan, plan.take, plan.turns - 1, blocks, pick).astype(jnp.float32)
    else:
        stats = [before_ref[b] for b in range(before_ref.shape[0])] + stats
        lane = lax.broadcasted_iota(jnp.int32, (2, 128), 1)
        codes = [plan.packed(plan.place, half) for half in range(2)]
        for j in range(plan.turns):
            halves = []
            for half in range(2):
                index = entry(codes[half], j)
                value = stats[0]
                for m in range(1, len(stats)):
                    value = jnp.where(index == m, stats[m], value)
                halves.append(value)
            stat_ref[:, j * 128:(j + 1) * 128] = jnp.where(lane < 64, halves[0], halves[1])


def score_call(plan, turns, comes, known, depth, squares=None, factor=None, before=None, kept=None):
    rows = comes[0].shape[0]
    first = squares is not None
    n = len(turns)
    stat = (n, 2, 128) if first else (2, plan.turns * 128)
    args = list(comes) + (list(squares) if first else [factor, before, kept]) + [a for _, a in known]
    out_shape = [jax.ShapeDtypeStruct((n, rows, 128), jnp.float32), jax.ShapeDtypeStruct(stat, jnp.float32)]
    if first:
        out_shape.append(jax.ShapeDtypeStruct((rows, 1), jnp.float32))
        out_shape.append(jax.ShapeDtypeStruct((rows, 128), jnp.float32))
    return pl.pallas_call(
        functools.partial(score_kernel, plan, turns, known, first, depth),
        out_shape=out_shape,
        in_specs=[VMEM] * len(args),
        out_specs=[VMEM] * len(out_shape),
        scratch_shapes=[pltpu.VMEM((2, rows, 128), jnp.bfloat16)] if first else [],
        compiler_params=pltpu.CompilerParams(vmem_limit_bytes=8 * 1024 * 1024),
        cost_estimate=pl.CostEstimate(flops=8 * n * rows * 128, bytes_accessed=12 * n * rows * 128, transcendentals=0),
    )(*args)


def arrange_kernel(plan, early_ref, late_ref, out_ref):
    lane = lax.broadcasted_iota(jnp.int32, late_ref.shape[1:], 1)
    codes = [plan.packed(plan.place, half) for half in range(2)]
    early = early_ref.shape[0]
    for j in range(plan.turns):
        halves = []
        for half in range(2):
            index = entry(codes[half], j)
            value = early_ref[jnp.minimum(index, early - 1)]
            halves.append(jnp.where(index < early, value, late_ref[0]))
        out_ref[:, j * 128:(j + 1) * 128] = jnp.where(lane < 64, halves[0], halves[1])


def arrange_call(plan, early, late):
    rows, width = late.shape[1], plan.turns * 128
    return pl.pallas_call(
        functools.partial(arrange_kernel, plan),
        out_shape=jax.ShapeDtypeStruct((rows, width), jnp.float32),
        in_specs=[VMEM] * 2,
        out_specs=VMEM,
        compiler_params=pltpu.CompilerParams(vmem_limit_bytes=8 * 1024 * 1024),
        cost_estimate=pl.CostEstimate(flops=rows * width, bytes_accessed=8 * rows * width, transcendentals=0),
    )(early, late)


def finish_kernel(count, stat_ref, come_ref, scored_ref, out_ref, held, sem):
    gap = come_ref[0:1, :] - stat_ref[0:1, :]
    mean = 0.5 * (stat_ref[0:1, :] + come_ref[0:1, :])
    spread = stat_ref[1:2, :] + come_ref[1:2, :] + (0.25 * count) * (gap * gap)
    scale = lax.rsqrt(spread / count + VAR_EPS)
    steps, rows = held.shape[0], held.shape[1]
    copies = []
    for i in range(steps):
        here = slice(i * rows, (i + 1) * rows)
        held[i] = ((scored_ref[here, :] - mean) * scale).astype(jnp.bfloat16)
        copies.append(pltpu.make_async_copy(held.at[i], out_ref.at[pl.ds(i * rows, rows)], sem.at[i]))
        copies[i].start()
    for copy in copies:
        copy.wait()


def finish_call(count, stat, come, scored, steps=2):
    rows, width = scored.shape
    return pl.pallas_call(
        functools.partial(finish_kernel, count),
        out_shape=jax.ShapeDtypeStruct((rows, width), jnp.bfloat16),
        in_specs=[VMEM] * 3,
        out_specs=pl.BlockSpec(memory_space=pltpu.HBM),
        scratch_shapes=[
            pltpu.VMEM((steps, rows // steps, width), jnp.bfloat16),
            pltpu.SemaphoreType.DMA((steps,)),
        ],
        compiler_params=pltpu.CompilerParams(vmem_limit_bytes=8 * 1024 * 1024),
        cost_estimate=pl.CostEstimate(flops=2 * rows * width, bytes_accessed=6 * rows * width, transcendentals=0),
    )(stat, come, scored)


def product_groups(plan):
    groups, p, m = [], 0, 0
    while p < plan.pairs:
        ready = max(max(plan.options(plan.give, half, m)) for half in range(2))
        n = 2 if p + 1 < ready and p + 1 < plan.pairs else 1
        done = p + n > ready
        groups.append((p, n, m if done else None))
        m += done
        p += n
    return groups


def ring_body(planes, gradients, queries, loss_weight):
    plan = Plan(planes)
    nodes, far = plan.nodes, plan.far
    rows_here, depth = gradients.shape
    feature_count = depth * 2

    def device(node, c):
        z, x = plan.order[node % nodes]
        return (z * 2 + x) * 2 + c

    swap = [(r, r ^ 1) for r in range(2 * nodes)]
    turn = [(device(n, n % 2), device(n + 1, (n + 1) % 2)) for n in range(nodes)]
    turn += [(device(n, 1 - n % 2), device(n - 1, n % 2)) for n in range(nodes)]

    def cross(value):
        return lax.ppermute(value, "feat", [(0, 1), (1, 0)])

    ring = [queries, lax.ppermute(queries, "rows", swap)]
    for _ in range(1, 2 * far):
        ring.append(lax.ppermute(ring[-2], "rows", turn))
    arrived = [([queries, ring[1]], [True, False])]
    for k in range(1, 2 * far):
        same = [(k + 1) // 2 % 2 == 0, (k + 1) // 2 % 2 == 1]
        arrived.append(([ring[k + 1], lax.ppermute(ring[k + 1], "rows", swap)], same if k % 2 else same[::-1]))

    gradients, squares = load_call(gradients)
    squares = (squares, cross(squares), loss_weight.reshape(rows_here // 128, 128))

    known, comes = [], []
    for p, n, m in product_groups(plan):
        units, sources = [], []
        for u, s in arrived[p:p + n]:
            units, sources = units + u, sources + s
        out = product_call(plan, gradients, units, sources, known, m)
        known.append((n, out[0]))
        if m is not None:
            comes.append(cross(out[2]))
        gradients = out[1]
    last = len(comes) - 1
    early, stat, factor, kept = score_call(plan, list(range(last)), comes[:last], known, feature_count, squares)
    late, stat = score_call(plan, [last], comes[last:], [], feature_count, None, factor, stat, kept)

    scored = arrange_call(plan, early, late)
    mean, spread = stat[0:1], stat[1:2]
    count, step = rows_here, 1
    while step < 2 * nodes:
        pairs = [(r, r ^ (step | 1)) for r in range(2 * nodes)]
        both = jnp.concatenate([mean, spread], axis=0)
        come = lax.ppermute(both, "rows", pairs)
        gap = come[0:1] - mean
        mean = 0.5 * (mean + come[0:1])
        spread = spread + come[1:2] + (0.5 * count) * (gap * gap)
        count *= 2
        step *= 2
    return finish_call(count, both, come, scored)


def solution(mesh):
    in_specs = (P("rows", "feat"), P("rows", "feat"), P("rows"))
    out_specs = P("rows", "feat")
    rows, feat = mesh.shape["rows"], mesh.shape["feat"]
    planes = rows // 4
    fits = rows == 4 * planes and planes in (2, 4) and feat == 2

    def body(gradients, queries, loss_weight):
        if fits and 2 * queries.shape[0] == 128 and gradients.shape[0] % 256 == 0:
            return ring_body(planes, gradients, queries, loss_weight)
        return plain_body(gradients, queries, loss_weight)

    return jax.shard_map(body, mesh=mesh, in_specs=in_specs, out_specs=out_specs, check_vma=False)
```
